256 devices in a mesh: row: 8 (over z), col: 16 (over x_hi, y, core), pan: 2 (over x_lo).
Axes of the slice: x: 4 (x_hi: 2, x_lo: 2; x = x_hi * 2 + x_lo), y: 4, z: 8, core: 2. Of those that a mesh axis runs over, the one named last changes fastest.
Arguments:
- gradient: bfloat16 [8192, 28672], P('row', ('col', 'pan')), may hold values from -240 to 240
- stat_old: float32 [8192, 1024], P(('row', 'col', 'pan')), may hold values from -4800 to 4800, as said below
Outputs:
- preconditioned: float32 [8192, 28672], P('row', ('col', 'pan'))
- stat_new: float32 [8192, 1024], P(('row', 'col', 'pan'))
The draws below stay inside these ranges and needn't reach their ends.
Inputs may be any that keep to these rules, and one draw needn't show every extreme that they name: Each block of 1024 rows of stat_old is a symmetric positive definite matrix.
All inputs are finite; a program needn't handle non-finite values.
Results may differ from the reference program's by a relative error of at most 0.0003.
Values sent between devices are 32-bit elements; how exact they have to be, the bound alone decides.
No kernel may reach another device: no remote copies, remote signals or barrier semaphores. Data moves between devices by JAX's collectives and lax.ppermute only.
A program may use at most 64 MiB of HBM per device.

```python
import math
import jax
import jax.numpy as jnp
from jax import lax

ORDER = 1024
COLS = 28672
ROWS = 8192


def shared_rows(key):
    picks = jax.random.randint(jax.random.fold_in(key, 11), (ROWS, 64), -2, 3)
    return picks.astype(jnp.float32)


def draw_gradient(key, part):
    key_rows, key_cols, key_body = jax.random.split(key, 3)
    row_pos = (jnp.arange(ROWS) % ORDER).astype(jnp.float32)
    row_scale = jnp.exp(jax.random.uniform(key_rows, (ROWS,), minval=math.log(0.3), maxval=math.log(3.0)))
    row_scale = row_scale * jnp.sqrt(1.0 + 2.0 * row_pos / (ORDER - 1))
    col_pos = jnp.arange(COLS).astype(jnp.float32)
    col_scale = jnp.exp(jax.random.uniform(key_cols, (COLS,), minval=math.log(0.5), maxval=math.log(2.0)))
    col_scale = col_scale * jnp.sqrt(1.0 + 2.0 * col_pos / (COLS - 1))
    mixing = jax.random.randint(jax.random.fold_in(key, 13), (64, COLS), -2, 3).astype(jnp.float32)
    shared = jnp.dot(shared_rows(key), mixing, precision=lax.Precision.HIGHEST) / 16.0
    values = shared + jnp.clip(jax.random.normal(key_body, (ROWS, COLS)), -4.0, 4.0)
    values = jnp.clip(values, -8.0, 8.0)
    return (row_scale[:, None] * col_scale[None, :] * values).astype(jnp.bfloat16)


def draw_stat_old(key, part):
    key_rows, key_body, key_mix = jax.random.split(jax.random.fold_in(key, 7), 3)
    blocks = ROWS // ORDER
    inner = 2048
    row_pos = (jnp.arange(ROWS) % ORDER).astype(jnp.float32)
    row_scale = jnp.exp(jax.random.uniform(key_rows, (ROWS,), minval=math.log(0.3), maxval=math.log(3.0)))
    row_scale = row_scale * jnp.sqrt(1.0 + 2.0 * row_pos / (ORDER - 1))
    rows_shared = shared_rows(key).reshape(blocks, ORDER, 64)
    mixing = jax.random.randint(key_mix, (blocks, 64, inner), -2, 3).astype(jnp.float32)
    shared = jnp.einsum('bir,brk->bik', rows_shared, mixing, precision=lax.Precision.HIGHEST) / 16.0
    noise = jnp.clip(jax.random.normal(key_body, (blocks, ORDER, inner)), -4.0, 4.0)
    values = jnp.clip(shared + noise, -8.0, 8.0)
    factors = row_scale.reshape(blocks, ORDER, 1) * values
    grams = jnp.einsum('bik,bjk->bij', factors, factors, precision=lax.Precision.HIGHEST) / inner
    grams = 0.5 * (grams + jnp.swapaxes(grams, 1, 2)) + 0.05 * jnp.eye(ORDER, dtype=jnp.float32)[None]
    return grams.reshape(ROWS, ORDER).astype(jnp.float32)


def setup_inputs(seed: int = 0) -> dict:
    key_list = jax.random.split(jax.random.key(seed), 3)
    gradient = draw_gradient(jax.random.fold_in(key_list[2], 71), 0)
    stat_old = draw_stat_old(jax.random.fold_in(key_list[2], 71), 0)
    return {"gradient": gradient, "stat_old": stat_old}


damping = 0.001
stat_decay = 0.9
newton_scale = 2.5

def block_step(gradient_block, old_block):
    highest = lax.Precision.HIGHEST
    grad_wide = gradient_block.astype(jnp.float32)
    gram = jnp.dot(grad_wide, grad_wide.T, precision=highest)
    stat_block = stat_decay * old_block + (1.0 - stat_decay) / COLS * gram
    order_size = old_block.shape[0]
    identity = jnp.eye(order_size, dtype=jnp.float32)
    matrix = stat_block + damping * identity
    frobenius = jnp.sqrt(jnp.sum(matrix * matrix))
    scaled = newton_scale * matrix / frobenius
    first_step = 1.25 * identity - 0.25 * scaled
    square = jnp.dot(first_step, first_step, precision=highest)
    fourth = jnp.dot(square, square, precision=highest)
    moved = jnp.dot(fourth, scaled, precision=highest)
    second_step = 1.25 * identity - 0.25 * moved
    product = jnp.dot(first_step, second_step, precision=highest)
    root = (frobenius / newton_scale) ** (-0.25) * product
    result = jnp.dot(root, grad_wide, precision=highest)
    return (result, stat_block)

def reference(gradient, stat_old):
    blocks = ROWS // ORDER
    grad_blocks = gradient.reshape(blocks, ORDER, COLS)
    old_blocks = stat_old.reshape(blocks, ORDER, ORDER)
    outputs = lax.map(lambda pair: block_step(pair[0], pair[1]), (grad_blocks, old_blocks))
    return (outputs[0].reshape(ROWS, COLS), outputs[1].reshape(ROWS, ORDER))
```

```python
import jax
import jax.numpy as jnp
from jax import lax
from jax.experimental import pallas as pl
from jax.experimental.pallas import tpu as pltpu
from jax.sharding import Mesh, PartitionSpec as P

COLS = 28672
ORDER = 1024
BIG = 256
SUB = 128
HALF = 18 * SUB

damping = 0.001
stat_decay = 0.9
newton_scale = 2.5
weight_new = (1.0 - stat_decay) / COLS

PLANE = ("xh", "y", "core", "xl")
CHIPS = ("xh", "y", "xl")
PARTNER = [(i, i ^ 2) for i in range(32)]


def diag_block(half, d):
    return 2 * half + d


def off_block(half, e):
    row = half * (1 + e // 2)
    col = jnp.where(half == 0, e + 1, min(e + 2, 3))
    return row, col


def gram_kernel(flip, grad_ref, old_ref, out_ref):
    core = lax.axis_index("core")
    half = jnp.bitwise_xor(core, flip)
    panel = (lax.axis_index("xh") * 16 + lax.axis_index("y") * 4 + core * 2 + lax.axis_index("xl"))
    old_big = panel // 8
    old_row = pl.multiple_of((panel % 4) * 32, 32)
    old_sub = (panel // 4) % 2

    def block(row, col):
        a = grad_ref[pl.ds(pl.multiple_of(row * BIG, BIG), BIG), :]
        b = grad_ref[pl.ds(pl.multiple_of(col * BIG, BIG), BIG), :]
        return weight_new * lax.dot_general(
            a, b, (((1,), (1,)), ((), ())), preferred_element_type=jnp.float32
        )

    def put(base, row, col, subs):
        value = block(row, col)
        for k, (i, j) in enumerate(subs):
            out_ref[(base + k) * SUB:(base + k + 1) * SUB, :] = value[
                i * SUB:(i + 1) * SUB, j * SUB:(j + 1) * SUB
            ]
        for k, (i, j) in enumerate(subs):

            @pl.when(jnp.logical_and(old_big == row, old_sub == i))
            def _():
                where = pl.ds((base + k) * SUB + old_row, 32)
                cols = pl.ds(pl.multiple_of(col * BIG + j * SUB, SUB), SUB)
                out_ref[where, :] += stat_decay * old_ref[:, cols]

    for d in range(2):
        at = diag_block(half, d)
        put(3 * d, at, at, [(0, 0), (0, 1), (1, 1)])
    for e in range(3):
        row, col = off_block(half, e)
        put(6 + 4 * e, row, col, [(0, 0), (0, 1), (1, 0), (1, 1)])


def split(value):
    high = value.astype(jnp.bfloat16)
    return high, (value - high.astype(jnp.float32)).astype(jnp.bfloat16)


def root_kernel(own_ref, other_ref, grad_ref, out_ref, stat_ref,
                mat, f_hi, f_lo, q_hi, q_lo, t_hi, t_lo):
    core = lax.axis_index("core")
    panel = (lax.axis_index("xh") * 16 + lax.axis_index("y") * 4 + core * 2 + lax.axis_index("xl"))
    eye_sub = (
        lax.broadcasted_iota(jnp.int32, (SUB, SUB), 0)
        == lax.broadcasted_iota(jnp.int32, (SUB, SUB), 1)
    ).astype(jnp.float32)

    def place(row, col):
        return (
            pl.ds(pl.multiple_of(row * SUB, SUB), SUB),
            pl.ds(pl.multiple_of(col * SUB, SUB), SUB),
        )

    total = jnp.zeros((SUB, SUB), jnp.float32)
    for ref, half in ((own_ref, core), (other_ref, 1 - core)):
        for d in range(2):
            at = diag_block(half, d)
            for k, (i, j) in enumerate([(0, 0), (0, 1), (1, 1)]):
                value = ref[(3 * d + k) * SUB:(3 * d + k + 1) * SUB, :]
                rows, cols = place(2 * at + i, 2 * at + j)
                mat[rows, cols] = value
                if i != j:
                    rows, cols = place(2 * at + j, 2 * at + i)
                    mat[rows, cols] = value.T
                    total += 2.0 * value * value
                else:
                    damped = value + damping * eye_sub
                    total += damped * damped
        for e in range(3):
            row, col = off_block(half, e)
            for k, (i, j) in enumerate([(0, 0), (0, 1), (1, 0), (1, 1)]):
                base = 6 + 4 * e + k
                value = ref[base * SUB:(base + 1) * SUB, :]
                rows, cols = place(2 * row + i, 2 * col + j)
                mat[rows, cols] = value
                rows, cols = place(2 * col + j, 2 * row + i)
                mat[rows, cols] = value.T
                total += 2.0 * value * value
    stat_ref[...] = mat[pl.ds(pl.multiple_of(panel * 32, 32), 32), :]
    sums = jnp.sum(jnp.sum(total, axis=0, keepdims=True), axis=1, keepdims=True)
    frobenius = jnp.sqrt(sums)
    factor = 0.25 * newton_scale / frobenius
    scale = 1.0 / jnp.sqrt(jnp.sqrt(frobenius / newton_scale))

    eye_big = (
        lax.broadcasted_iota(jnp.int32, (BIG, BIG), 0)
        == lax.broadcasted_iota(jnp.int32, (BIG, BIG), 1)
    ).astype(jnp.float32)

    def big(i):
        return slice(i * BIG, (i + 1) * BIG)

    for i in range(4):
        for j in range(4):
            value = -factor * mat[big(i), big(j)]
            if i == j:
                value += (1.25 - factor * damping) * eye_big
            mat[big(i), big(j)] = value
            f_hi[big(i), big(j)], f_lo[big(i), big(j)] = split(value)

    def triple(a_hi, a_lo, b_hi, b_lo, j):
        rows = slice(0, (j + 1) * BIG)
        return (
            jnp.dot(a_hi[rows, :], b_hi[:, big(j)], preferred_element_type=jnp.float32)
            + jnp.dot(a_hi[rows, :], b_lo[:, big(j)], preferred_element_type=jnp.float32)
            + jnp.dot(a_lo[rows, :], b_hi[:, big(j)], preferred_element_type=jnp.float32)
        )

    def store(hi, lo, i, j, value):
        hi[big(i), big(j)], lo[big(i), big(j)] = split(value)
        if i != j:
            hi[big(j), big(i)], lo[big(j), big(i)] = split(value.T)

    for j in range(4):
        value = triple(f_hi, f_lo, f_hi, f_lo, j)
        for i in range(j + 1):
            part = value[big(i), :]
            store(q_hi, q_lo, i, j, part)
            store(t_hi, t_lo, i, j, 1.25 * mat[big(i), big(j)] - part)
    for j in range(4):
        value = triple(q_hi, q_lo, q_hi, q_lo, j)
        for i in range(j + 1):
            store(f_hi, f_lo, i, j, value[big(i), :])
    for j in range(4):
        value = triple(f_hi, f_lo, t_hi, t_lo, j)
        for i in range(j + 1):
            part = scale * (1.25 * mat[big(i), big(j)] - value[big(i), :])
            store(q_hi, q_lo, i, j, part)
    for i in range(4):
        out_ref[big(i), :] = jnp.dot(
            q_hi[big(i), :], grad_ref[...], preferred_element_type=jnp.float32
        ) + jnp.dot(q_lo[big(i), :], grad_ref[...], preferred_element_type=jnp.float32)


def local(gradient, stat_old):
    vmem = pl.BlockSpec(memory_space=pltpu.VMEM)

    def gram(flip):
        return pl.pallas_call(
            lambda *refs: gram_kernel(flip, *refs),
            out_shape=jax.ShapeDtypeStruct((HALF, SUB), jnp.float32),
            in_specs=[vmem, vmem],
            out_specs=vmem,
            name=f"gram{flip}",
        )(gradient, stat_old)

    theirs = gram(1)
    arrived = lax.ppermute(theirs, PLANE, PARTNER)
    pair = gram(0) + arrived
    pieces = lax.all_to_all(pair.reshape(16, HALF // 16, SUB), CHIPS, 0, 0)
    piece = jnp.sum(pieces, axis=0)
    whole = lax.all_to_all(
        jnp.broadcast_to(piece[None], (16, HALF // 16, SUB)), CHIPS, 0, 0
    ).reshape(HALF, SUB)
    other = lax.ppermute(whole, PLANE, PARTNER)
    square = (ORDER, ORDER)
    return pl.pallas_call(
        root_kernel,
        out_shape=(
            jax.ShapeDtypeStruct(gradient.shape, jnp.float32),
            jax.ShapeDtypeStruct(stat_old.shape, jnp.float32),
        ),
        in_specs=[vmem, vmem, vmem],
        out_specs=(vmem, vmem),
        scratch_shapes=[pltpu.VMEM(square, jnp.float32)]
        + [pltpu.VMEM(square, jnp.bfloat16)] * 6,
        name="root",
    )(whole, other, gradient)


def solution(mesh):
    fine = Mesh(mesh.devices.reshape(8, 2, 4, 2, 2), ("row",) + PLANE)
    placed = (P("row", PLANE), P(("row",) + PLANE, None))
    return jax.shard_map(
        local, mesh=fine, in_specs=placed, out_specs=placed, check_vma=False
    )
```

```python
import jax
import jax.numpy as jnp
from jax import lax
from jax.experimental import pallas as pl
from jax.experimental.pallas import tpu as pltpu
from jax.sharding import Mesh, PartitionSpec as P

COLS = 28672
ORDER = 1024
BIG = 256
SUB = 128
CHUNK = 2 * BIG + 8

damping = 0.001
stat_decay = 0.9
newton_scale = 2.5
weight_new = (1.0 - stat_decay) / COLS

ORIGINS = (0, 2, 1, 3)
PLANE = ("xh", "y", "core", "xl")


def pairs(first, second, other):
    found = []
    for x in range(4):
        for y in range(4):
            for core in range(2):
                dx, dy = (second, first) if core else (first, second)
                ends = []
                for u, v, w in ((x, y, core), ((x + dx) % 4, (y + dy) % 4, core ^ other)):
                    ends.append(((u // 2 * 4 + v) * 2 + w) * 2 + u % 2)
                found.append(tuple(ends))
    return found


def position():
    places = lax.axis_index("xh") * 2 + lax.axis_index("xl"), lax.axis_index("y")
    core = lax.axis_index("core")
    panel = (
        lax.axis_index("xh") * 16 + lax.axis_index("y") * 4 + core * 2 + lax.axis_index("xl")
    )
    return places, core, panel


def off_block(half, which):
    row = jnp.where(half == 0, 0, jnp.where(which == 3, 2, 1))
    col = jnp.where(half == 0, which, jnp.where(which == 1, 2, 3))
    return row, col


def sub_masks():
    rows = lax.broadcasted_iota(jnp.int32, (SUB, SUB), 0)
    cols = lax.broadcasted_iota(jnp.int32, (SUB, SUB), 1)
    return rows <= cols, rows == cols


def gram_kernel(flip, grad_ref, old_ref, out_ref, block_ref):
    places, core, panel = position()
    half = jnp.bitwise_xor(core, flip)
    place = jnp.where(half == 0, places[0], places[1])
    old_big = panel // 8
    old_row = pl.multiple_of((panel % 8) * 32, 32)
    upper, diagonal = sub_masks()

    def block(row, col):
        a = grad_ref[pl.ds(pl.multiple_of(row * BIG, BIG), BIG), :]
        b = grad_ref[pl.ds(pl.multiple_of(col * BIG, BIG), BIG), :]
        return weight_new * lax.dot_general(
            a, b, (((1,), (1,)), ((), ())), preferred_element_type=jnp.float32
        )

    def old(col, part):
        return stat_decay * old_ref[:, pl.ds(pl.multiple_of(col * BIG + part * SUB, SUB), SUB)]

    for k in range(4):
        which = (place + k) % 4

        @pl.when(which == 0)
        def _():
            extra = []
            for d in range(2):
                at = 2 * half + d
                block_ref[...] = block(at, at)

                @pl.when(old_big == at)
                def _():
                    for part in range(2):
                        cols = slice(part * SUB, (part + 1) * SUB)
                        block_ref[pl.ds(old_row, 32), cols] += old(at, part)

                out_ref[k, 2 * d * SUB:(2 * d + 1) * SUB, :] = block_ref[:SUB, SUB:]
                second = block_ref[SUB:, SUB:]
                out_ref[k, (2 * d + 1) * SUB:(2 * d + 2) * SUB, :] = jnp.where(
                    upper, block_ref[:SUB, :SUB], second
                )
                extra.append(jnp.sum(jnp.where(diagonal, second, 0.0), axis=0, keepdims=True))
            out_ref[k, 2 * BIG:, :] = jnp.concatenate(
                extra + [jnp.zeros((6, SUB), jnp.float32)], axis=0
            )

        @pl.when(which != 0)
        def _():
            row, col = off_block(half, which)
            value = block(row, col)
            for part in range(2):
                out_ref[k, part * BIG:(part + 1) * BIG, :] = value[
                    :, part * SUB:(part + 1) * SUB
                ]

            @pl.when(old_big == row)
            def _():
                for part in range(2):
                    out_ref[k, pl.ds(part * BIG + old_row, 32), :] += old(col, part)

            out_ref[k, 2 * BIG:, :] = jnp.zeros((8, SUB), jnp.float32)


def split(value):
    high = value.astype(jnp.bfloat16)
    return high, (value - high.astype(jnp.float32)).astype(jnp.bfloat16)


def root_kernel(*refs):
    chunks = refs[:8]
    grad_hbm, out_hbm, stat_ref = refs[8:11]
    mat, f_hi, f_lo, q_hi, q_lo, t_hi, t_lo, total, grad_ref, out_ref, sem_in, sem_out = refs[11:]
    load = pltpu.make_async_copy(grad_hbm, grad_ref, sem_in)
    load.start()
    places, core, panel = position()
    upper, diagonal = sub_masks()
    total[...] = jnp.zeros((SUB, SUB), jnp.float32)

    def at_big(row, part=0):
        return pl.ds(pl.multiple_of(row * BIG + part * SUB, SUB), SUB)

    def whole_big(row):
        return pl.ds(pl.multiple_of(row * BIG, BIG), BIG)

    for n, ref in enumerate(chunks):
        half = jnp.bitwise_xor(core, n // 4)
        which = (jnp.where(half == 0, places[0], places[1]) + 4 - ORIGINS[n % 4]) % 4

        @pl.when(which == 0)
        def _():
            for d in range(2):
                at = 2 * half + d
                value = ref[2 * d * SUB:(2 * d + 1) * SUB, :]
                mat[at_big(at), at_big(at, 1)] = value
                mat[at_big(at, 1), at_big(at)] = value.T
                both = ref[(2 * d + 1) * SUB:(2 * d + 2) * SUB, :]
                flipped = both.T
                first = jnp.where(upper, both, flipped)
                second = jnp.where(
                    diagonal,
                    jnp.broadcast_to(ref[2 * BIG + d:2 * BIG + d + 1, :], (SUB, SUB)),
                    jnp.where(upper, flipped, both),
                )
                mat[at_big(at), at_big(at)] = first
                mat[at_big(at, 1), at_big(at, 1)] = second
                damp = jnp.where(diagonal, damping, 0.0)
                first += damp
                second += damp
                total[...] += 2.0 * value * value + first * first + second * second

        @pl.when(which != 0)
        def _():
            row, col = off_block(half, which)
            for part in range(2):
                value = ref[part * BIG:(part + 1) * BIG, :]
                mat[whole_big(row), at_big(col, part)] = value
                mat[at_big(col, part), whole_big(row)] = value.T
                squared = 2.0 * value * value
                total[...] += squared[:SUB] + squared[SUB:]

    stat_ref[...] = mat[pl.ds(pl.multiple_of(panel * 32, 32), 32), :]
    sums = jnp.sum(jnp.sum(total[...], axis=0, keepdims=True), axis=1, keepdims=True)
    frobenius = jnp.sqrt(sums)
    factor = 0.25 * newton_scale / frobenius
    scale = 1.0 / jnp.sqrt(jnp.sqrt(frobenius / newton_scale))

    eye_big = (
        lax.broadcasted_iota(jnp.int32, (BIG, BIG), 0)
        == lax.broadcasted_iota(jnp.int32, (BIG, BIG), 1)
    ).astype(jnp.float32)

    def big(i):
        return slice(i * BIG, (i + 1) * BIG)

    for i in range(4):
        for j in range(4):
            value = -factor * mat[big(i), big(j)]
            if i == j:
                value += (1.25 - factor * damping) * eye_big
            mat[big(i), big(j)] = value
            f_hi[big(i), big(j)], f_lo[big(i), big(j)] = split(value)

    def triple(a_hi, a_lo, b_hi, b_lo, j):
        rows = slice(0, (j + 1) * BIG)
        return (
            jnp.dot(a_hi[rows, :], b_hi[:, big(j)], preferred_element_type=jnp.float32)
            + jnp.dot(a_hi[rows, :], b_lo[:, big(j)], preferred_element_type=jnp.float32)
            + jnp.dot(a_lo[rows, :], b_hi[:, big(j)], preferred_element_type=jnp.float32)
        )

    def store(hi, lo, i, j, value):
        hi[big(i), big(j)], lo[big(i), big(j)] = split(value)
        if i != j:
            hi[big(j), big(i)], lo[big(j), big(i)] = split(value.T)

    for j in range(4):
        value = triple(f_hi, f_lo, f_hi, f_lo, j)
        for i in range(j + 1):
            part = value[big(i), :]
            store(q_hi, q_lo, i, j, part)
            store(t_hi, t_lo, i, j, 1.25 * mat[big(i), big(j)] - part)
    for j in range(4):
        value = triple(q_hi, q_lo, q_hi, q_lo, j)
        for i in range(j + 1):
            store(f_hi, f_lo, i, j, value[big(i), :])
    for j in range(4):
        value = triple(f_hi, f_lo, t_hi, t_lo, j)
        for i in range(j + 1):
            part = scale * (1.25 * mat[big(i), big(j)] - value[big(i), :])
            store(q_hi, q_lo, i, j, part)
    load.wait()
    copies = []
    for i in range(4):
        out_ref[big(i), :] = jnp.dot(
            q_hi[big(i), :], grad_ref[...], preferred_element_type=jnp.float32
        ) + jnp.dot(q_lo[big(i), :], grad_ref[...], preferred_element_type=jnp.float32)
        copies.append(
            pltpu.make_async_copy(out_ref.at[big(i), :], out_hbm.at[big(i), :], sem_out.at[i])
        )
        copies[-1].start()
    for copy in copies:
        copy.wait()


def local(gradient, stat_old):
    vmem = pl.BlockSpec(memory_space=pltpu.VMEM)
    anywhere = pl.BlockSpec(memory_space=pl.ANY)

    def gram(flip):
        return pl.pallas_call(
            lambda *refs: gram_kernel(flip, *refs),
            out_shape=jax.ShapeDtypeStruct((4, CHUNK, SUB), jnp.float32),
            in_specs=[vmem, vmem],
            out_specs=vmem,
            scratch_shapes=[pltpu.VMEM((BIG, BIG), jnp.float32)],
            name=f"gram{flip}",
        )(gradient, stat_old)

    def move(value, first=0, second=0, other=0):
        return lax.ppermute(value, PLANE, pairs(first, second, other))

    arrived = move(gram(1), other=1)
    own = gram(0)
    sums = [own[k] + arrived[k] for k in range(4)]
    for k in (2, 1, 3):
        sums[k] = move(sums[k], first=k)
    chunk = (sums[0] + sums[1]) + (sums[2] + sums[3])
    others = [move(chunk, second=k) for k in (2, 1, 3)]
    chunk = (chunk + others[0]) + (others[1] + others[2])
    mine = [chunk] + [move(chunk, first=k) for k in (2, 1, 3)]
    theirs = [move(value, other=1) for value in mine]

    square = (ORDER, ORDER)
    return pl.pallas_call(
        root_kernel,
        out_shape=(
            jax.ShapeDtypeStruct(gradient.shape, jnp.float32),
            jax.ShapeDtypeStruct(stat_old.shape, jnp.float32),
        ),
        in_specs=[vmem] * 8 + [anywhere],
        out_specs=(anywhere, vmem),
        scratch_shapes=[pltpu.VMEM(square, jnp.float32)]
        + [pltpu.VMEM(square, jnp.bfloat16)] * 6
        + [
            pltpu.VMEM((SUB, SUB), jnp.float32),
            pltpu.VMEM(gradient.shape, jnp.bfloat16),
            pltpu.VMEM(gradient.shape, jnp.float32),
            pltpu.SemaphoreType.DMA,
            pltpu.SemaphoreType.DMA((4,)),
        ],
        name="root",
    )(*mine, *theirs, gradient)


def solution(mesh):
    fine = Mesh(mesh.devices.reshape(8, 2, 4, 2, 2), ("row",) + PLANE)
    placed = (P("row", PLANE), P(("row",) + PLANE, None))
    return jax.shard_map(
        local, mesh=fine, in_specs=placed, out_specs=placed, check_vma=False
    )
```

```python
import jax
import jax.numpy as jnp
from jax import lax
from jax.experimental import pallas as pl
from jax.experimental.pallas import tpu as pltpu
from jax.sharding import Mesh, PartitionSpec as P

COLS = 28672
ORDER = 1024
BIG = 256
SUB = 128
CHUNK = 2 * BIG + 8

damping = 0.001
stat_decay = 0.9
newton_scale = 2.5
weight_new = (1.0 - stat_decay) / COLS

ORIGINS = (0, 2, 1, 3)
PLANE = ("xh", "y", "core", "xl")


def pairs(first, second, other):
    found = []
    for x in range(4):
        for y in range(4):
            for core in range(2):
                dx, dy = (second, first) if core else (first, second)
                ends = []
                for u, v, w in ((x, y, core), ((x + dx) % 4, (y + dy) % 4, core ^ other)):
                    ends.append(((u // 2 * 4 + v) * 2 + w) * 2 + u % 2)
                found.append(tuple(ends))
    return found


def position():
    places = lax.axis_index("xh") * 2 + lax.axis_index("xl"), lax.axis_index("y")
    core = lax.axis_index("core")
    panel = (
        lax.axis_index("xh") * 16 + lax.axis_index("y") * 4 + core * 2 + lax.axis_index("xl")
    )
    return places, core, panel


def off_block(half, which):
    row = jnp.where(half == 0, 0, jnp.where(which == 3, 2, 1))
    col = jnp.where(half == 0, which, jnp.where(which == 1, 2, 3))
    return row, col


def sub_masks():
    rows = lax.broadcasted_iota(jnp.int32, (SUB, SUB), 0)
    cols = lax.broadcasted_iota(jnp.int32, (SUB, SUB), 1)
    return rows <= cols, rows == cols


def gram_kernel(flip, grad_ref, old_ref, out_ref, block_ref):
    places, core, panel = position()
    half = jnp.bitwise_xor(core, flip)
    place = jnp.where(half == 0, places[0], places[1])
    old_big = panel // 8
    old_row = pl.multiple_of((panel % 8) * 32, 32)
    upper, diagonal = sub_masks()

    def block(row, col):
        a = grad_ref[pl.ds(pl.multiple_of(row * BIG, BIG), BIG), :]
        b = grad_ref[pl.ds(pl.multiple_of(col * BIG, BIG), BIG), :]
        return weight_new * lax.dot_general(
            a, b, (((1,), (1,)), ((), ())), preferred_element_type=jnp.float32
        )

    def old(col, part):
        return stat_decay * old_ref[:, pl.ds(pl.multiple_of(col * BIG + part * SUB, SUB), SUB)]

    for k in range(4):
        which = (place + k) % 4

        @pl.when(which == 0)
        def _():
            extra = []
            for d in range(2):
                at = 2 * half + d
                block_ref[...] = block(at, at)

                @pl.when(old_big == at)
                def _():
                    for part in range(2):
                        cols = slice(part * SUB, (part + 1) * SUB)
                        block_ref[pl.ds(old_row, 32), cols] += old(at, part)

                out_ref[k, 2 * d * SUB:(2 * d + 1) * SUB, :] = block_ref[:SUB, SUB:]
                second = block_ref[SUB:, SUB:]
                out_ref[k, (2 * d + 1) * SUB:(2 * d + 2) * SUB, :] = jnp.where(
                    upper, block_ref[:SUB, :SUB], second
                )
                extra.append(jnp.sum(jnp.where(diagonal, second, 0.0), axis=0, keepdims=True))
            out_ref[k, 2 * BIG:, :] = jnp.concatenate(
                extra + [jnp.zeros((6, SUB), jnp.float32)], axis=0
            )

        @pl.when(which != 0)
        def _():
            row, col = off_block(half, which)
            value = block(row, col)
            for part in range(2):
                out_ref[k, part * BIG:(part + 1) * BIG, :] = value[
                    :, part * SUB:(part + 1) * SUB
                ]

            @pl.when(old_big == row)
            def _():
                for part in range(2):
                    out_ref[k, pl.ds(part * BIG + old_row, 32), :] += old(col, part)

            out_ref[k, 2 * BIG:, :] = jnp.zeros((8, SUB), jnp.float32)


def split(value):
    high = value.astype(jnp.bfloat16)
    return high, (value - high.astype(jnp.float32)).astype(jnp.bfloat16)


def root_kernel(*refs):
    chunks = refs[:8]
    grad_ref, out_hbm, stat_ref = refs[8:11]
    mat, cross, f_hi, f_lo, q_hi, q_lo, t_hi, t_lo, total, out_ref, sem_out = refs[11:]
    places, core, panel = position()
    upper, diagonal = sub_masks()
    total[...] = jnp.zeros((SUB, SUB), jnp.float32)

    def at_big(row, part=0):
        return pl.ds(pl.multiple_of(row * BIG + part * SUB, SUB), SUB)

    def whole_big(row):
        return pl.ds(pl.multiple_of(row * BIG, BIG), BIG)

    for n, ref in enumerate(chunks):
        half = jnp.bitwise_xor(core, n // 4)
        which = (jnp.where(half == 0, places[0], places[1]) + 4 - ORIGINS[n % 4]) % 4

        @pl.when(which == 0)
        def _():
            for d in range(2):
                at = 2 * half + d
                value = ref[2 * d * SUB:(2 * d + 1) * SUB, :]
                mat[at_big(at), at_big(at, 1)] = value
                mat[at_big(at, 1), at_big(at)] = value.T
                both = ref[(2 * d + 1) * SUB:(2 * d + 2) * SUB, :]
                flipped = both.T
                first = jnp.where(upper, both, flipped)
                second = jnp.where(
                    diagonal,
                    jnp.broadcast_to(ref[2 * BIG + d:2 * BIG + d + 1, :], (SUB, SUB)),
                    jnp.where(upper, flipped, both),
                )
                mat[at_big(at), at_big(at)] = first
                mat[at_big(at, 1), at_big(at, 1)] = second
                damp = jnp.where(diagonal, damping, 0.0)
                first += damp
                second += damp
                total[...] += 2.0 * value * value + first * first + second * second

        @pl.when(which != 0)
        def _():
            row, col = off_block(half, which)
            for part in range(2):
                value = ref[part * BIG:(part + 1) * BIG, :]
                mat[whole_big(row), at_big(col, part)] = value
                mat[at_big(col, part), whole_big(row)] = value.T
                squared = 2.0 * value * value
                total[...] += squared[:SUB] + squared[SUB:]

    stat_ref[...] = mat[pl.ds(pl.multiple_of(panel * 32, 32), 32), :]
    sums = jnp.sum(jnp.sum(total[...], axis=0, keepdims=True), axis=1, keepdims=True)
    frobenius = jnp.sqrt(sums)
    factor = 0.25 * newton_scale / frobenius
    scale = 1.0 / jnp.sqrt(jnp.sqrt(frobenius / newton_scale))

    eye_big = (
        lax.broadcasted_iota(jnp.int32, (BIG, BIG), 0)
        == lax.broadcasted_iota(jnp.int32, (BIG, BIG), 1)
    ).astype(jnp.float32)

    def big(i):
        return slice(i * BIG, (i + 1) * BIG)

    for i in range(4):
        for j in range(4):
            value = -factor * mat[big(i), big(j)]
            if i == j:
                value += (1.25 - factor * damping) * eye_big
            mat[big(i), big(j)] = value
            f_hi[big(i), big(j)], f_lo[big(i), big(j)] = split(value)

    def triple(a_hi, a_lo, b_hi, b_lo, j):
        rows = slice(0, (j + 1) * BIG)
        return (
            jnp.dot(a_hi[rows, :], b_hi[:, big(j)], preferred_element_type=jnp.float32)
            + jnp.dot(a_hi[rows, :], b_lo[:, big(j)], preferred_element_type=jnp.float32)
            + jnp.dot(a_lo[rows, :], b_hi[:, big(j)], preferred_element_type=jnp.float32)
        )

    def store(hi, lo, i, j, value):
        hi[big(i), big(j)], lo[big(i), big(j)] = split(value)
        if i != j:
            hi[big(j), big(i)], lo[big(j), big(i)] = split(value.T)

    def squared(hi, lo, done):
        for j in range(4):
            cross[:, big(j)] = jnp.dot(
                hi[...], lo[:, big(j)], preferred_element_type=jnp.float32
            )
        for j in range(4):
            value = jnp.dot(
                hi[:(j + 1) * BIG, :], hi[:, big(j)], preferred_element_type=jnp.float32
            )
            for i in range(j + 1):
                done(i, j, value[big(i), :] + (cross[big(i), big(j)] + cross[big(j), big(i)].T))

    def square_done(i, j, part):
        store(q_hi, q_lo, i, j, part)
        store(t_hi, t_lo, i, j, 1.25 * mat[big(i), big(j)] - part)

    squared(f_hi, f_lo, square_done)
    squared(q_hi, q_lo, lambda i, j, part: store(f_hi, f_lo, i, j, part))
    for j in range(4):
        value = triple(f_hi, f_lo, t_hi, t_lo, j)
        for i in range(j + 1):
            part = scale * (1.25 * mat[big(i), big(j)] - value[big(i), :])
            store(q_hi, q_lo, i, j, part)
    copies = []
    for i in range(4):
        out_ref[big(i), :] = jnp.dot(
            q_hi[big(i), :], grad_ref[...], preferred_element_type=jnp.float32
        ) + jnp.dot(q_lo[big(i), :], grad_ref[...], preferred_element_type=jnp.float32)
        copies.append(
            pltpu.make_async_copy(out_ref.at[big(i), :], out_hbm.at[big(i), :], sem_out.at[i])
        )
        copies[-1].start()
    for copy in copies:
        copy.wait()


def local(gradient, stat_old):
    vmem = pl.BlockSpec(memory_space=pltpu.VMEM)
    anywhere = pl.BlockSpec(memory_space=pl.ANY)

    def kept(value):
        return pltpu.with_memory_space_constraint(value, pltpu.VMEM)

    grad_kept, old_kept = kept(gradient), kept(stat_old)

    def gram(flip, name):
        return pl.pallas_call(
            lambda *refs: gram_kernel(flip, *refs),
            out_shape=pltpu.VMEM((4, CHUNK, SUB), jnp.float32),
            in_specs=[vmem, vmem],
            out_specs=vmem,
            scratch_shapes=[pltpu.VMEM((BIG, BIG), jnp.float32)],
            compiler_params=pltpu.CompilerParams(vmem_limit_bytes=8 << 20),
            name=name,
        )(grad_kept, old_kept)

    def move(value, first=0, second=0, other=0):
        return lax.ppermute(value, PLANE, pairs(first, second, other))

    arrived = move(gram(1, "gram_other"), other=1)
    own = gram(0, "gram_own")
    sums = [own[k] + arrived[k] for k in range(4)]
    for k in (2, 1, 3):
        sums[k] = move(sums[k], first=k)
    chunk = (sums[0] + sums[1]) + (sums[2] + sums[3])
    others = [move(chunk, second=k) for k in (2, 1, 3)]
    chunk = (chunk + others[0]) + (others[1] + others[2])
    mine = [chunk] + [move(chunk, first=k) for k in (2, 1, 3)]
    theirs = [move(value, other=1) for value in mine]

    square = (ORDER, ORDER)
    return pl.pallas_call(
        root_kernel,
        out_shape=(
            jax.ShapeDtypeStruct(gradient.shape, jnp.float32),
            jax.ShapeDtypeStruct(stat_old.shape, jnp.float32),
        ),
        in_specs=[vmem] * 9,
        out_specs=(anywhere, vmem),
        scratch_shapes=[pltpu.VMEM(square, jnp.float32)] * 2
        + [pltpu.VMEM(square, jnp.bfloat16)] * 6
        + [
            pltpu.VMEM((SUB, SUB), jnp.float32),
            pltpu.VMEM(gradient.shape, jnp.float32),
            pltpu.SemaphoreType.DMA((4,)),
        ],
        compiler_params=pltpu.CompilerParams(vmem_limit_bytes=44 << 20),
        name="root",
    )(*map(kept, mine + theirs), grad_kept)


def solution(mesh):
    fine = Mesh(mesh.devices.reshape(8, 2, 4, 2, 2), ("row",) + PLANE)
    placed = (P("row", PLANE), P(("row",) + PLANE, None))
    return jax.shard_map(
        local, mesh=fine, in_specs=placed, out_specs=placed, check_vma=False
    )
```

```python
import jax
import jax.numpy as jnp
from jax import lax
from jax.experimental import pallas as pl
from jax.experimental.pallas import tpu as pltpu
from jax.sharding import Mesh, PartitionSpec as P

COLS = 28672
ORDER = 1024
BIG = 256
SUB = 128
PARTS = (BIG, BIG + 8)

damping = 0.001
stat_decay = 0.9
newton_scale = 2.5
weight_new = (1.0 - stat_decay) / COLS

ORIGINS = (0, 2, 1, 3)
PLANE = ("xh", "y", "core", "xl")


def pairs(first, second, other):
    found = []
    for x in range(4):
        for y in range(4):
            for core in range(2):
                dx, dy = (second, first) if core else (first, second)
                ends = []
                for u, v, w in ((x, y, core), ((x + dx) % 4, (y + dy) % 4, core ^ other)):
                    ends.append(((u // 2 * 4 + v) * 2 + w) * 2 + u % 2)
                found.append(tuple(ends))
    return found


def position():
    places = lax.axis_index("xh") * 2 + lax.axis_index("xl"), lax.axis_index("y")
    core = lax.axis_index("core")
    panel = (
        lax.axis_index("xh") * 16 + lax.axis_index("y") * 4 + core * 2 + lax.axis_index("xl")
    )
    return places, core, panel


def off_block(half, which):
    row = jnp.where(half == 0, 0, jnp.where(which == 3, 2, 1))
    col = jnp.where(half == 0, which, jnp.where(which == 1, 2, 3))
    return row, col


def sub_masks():
    rows = lax.broadcasted_iota(jnp.int32, (SUB, SUB), 0)
    cols = lax.broadcasted_iota(jnp.int32, (SUB, SUB), 1)
    return rows <= cols, rows == cols


def load_kernel(grad_hbm, old_hbm, left_ref, right_ref, grad_ref, old_ref, blocks, sems):
    copies = [
        pltpu.make_async_copy(grad_hbm, grad_ref, sems.at[0]),
        pltpu.make_async_copy(old_hbm, old_ref, sems.at[1]),
    ]
    for copy in copies:
        copy.start()
    for copy in copies:
        copy.wait()
    gram_kernel(1, grad_ref, old_ref, left_ref, right_ref, blocks)


def gram_kernel(flip, grad_ref, old_ref, left_ref, right_ref, blocks):
    places, core, panel = position()
    half = jnp.bitwise_xor(core, flip)
    place = jnp.where(half == 0, places[0], places[1])
    old_big = panel // 8
    old_row = pl.multiple_of((panel % 8) * 32, 32)
    upper, diagonal = sub_masks()

    def big(index):
        return pl.ds(pl.multiple_of(index * BIG, BIG), BIG)

    which = [(place + k) % 4 for k in range(4)]
    where = []
    for k in range(4):
        row, col = off_block(half, which[k])
        where.append(tuple(jnp.where(which[k] == 0, 2 * half, v) for v in (row, col)))
    where.append((2 * half + 1, 2 * half + 1))
    for n, (row, col) in enumerate(where):
        blocks[n] = weight_new * lax.dot_general(
            grad_ref[big(row), :],
            grad_ref[big(col), :],
            (((1,), (1,)), ((), ())),
            preferred_element_type=jnp.float32,
        )
    for n, (row, col) in enumerate(where):

        @pl.when(old_big == row)
        def _():
            blocks[n, pl.ds(old_row, 32), :] += stat_decay * old_ref[:, big(col)]

    for k in range(4):

        @pl.when(which[k] == 0)
        def _():
            extra = []
            for n, ref in ((k, left_ref), (4, right_ref)):
                second = blocks[n, SUB:, SUB:]
                ref[k, :SUB, :] = blocks[n, :SUB, SUB:]
                ref[k, SUB:BIG, :] = jnp.where(upper, blocks[n, :SUB, :SUB], second)
                extra.append(jnp.sum(jnp.where(diagonal, second, 0.0), axis=0, keepdims=True))
            right_ref[k, BIG:, :] = jnp.concatenate(
                extra + [jnp.zeros((6, SUB), jnp.float32)], axis=0
            )

        @pl.when(which[k] != 0)
        def _():
            left_ref[k] = blocks[k, :, :SUB]
            right_ref[k, :BIG, :] = blocks[k, :, SUB:]
            right_ref[k, BIG:, :] = jnp.zeros((8, SUB), jnp.float32)


def split(value):
    high = value.astype(jnp.bfloat16)
    return high, (value - high.astype(jnp.float32)).astype(jnp.bfloat16)


def root_kernel(*refs):
    chunks = list(zip(refs[:8], refs[8:16]))
    grad_ref, out_hbm, stat_ref = refs[16:19]
    mat, cross, f_hi, f_lo, q_hi, q_lo, t_hi, t_lo, total, out_ref, sem_out = refs[19:]
    places, core, panel = position()
    upper, diagonal = sub_masks()
    total[...] = jnp.zeros((SUB, SUB), jnp.float32)

    def at_big(row, part=0):
        return pl.ds(pl.multiple_of(row * BIG + part * SUB, SUB), SUB)

    def whole_big(row):
        return pl.ds(pl.multiple_of(row * BIG, BIG), BIG)

    for n, parts in enumerate(chunks):
        half = jnp.bitwise_xor(core, n // 4)
        which = (jnp.where(half == 0, places[0], places[1]) + 4 - ORIGINS[n % 4]) % 4

        @pl.when(which == 0)
        def _():
            for d, ref in enumerate(parts):
                at = 2 * half + d
                value = ref[:SUB, :]
                mat[at_big(at), at_big(at, 1)] = value
                mat[at_big(at, 1), at_big(at)] = value.T
                both = ref[SUB:BIG, :]
                flipped = both.T
                first = jnp.where(upper, both, flipped)
                second = jnp.where(
                    diagonal,
                    jnp.broadcast_to(parts[1][BIG + d:BIG + d + 1, :], (SUB, SUB)),
                    jnp.where(upper, flipped, both),
                )
                mat[at_big(at), at_big(at)] = first
                mat[at_big(at, 1), at_big(at, 1)] = second
                damp = jnp.where(diagonal, damping, 0.0)
                first += damp
                second += damp
                total[...] += 2.0 * value * value + first * first + second * second

        @pl.when(which != 0)
        def _():
            row, col = off_block(half, which)
            for part, ref in enumerate(parts):
                value = ref[:BIG, :]
                mat[whole_big(row), at_big(col, part)] = value
                mat[at_big(col, part), whole_big(row)] = value.T
                both = 2.0 * value * value
                total[...] += both[:SUB] + both[SUB:]

    stat_ref[...] = mat[pl.ds(pl.multiple_of(panel * 32, 32), 32), :]
    sums = jnp.sum(jnp.sum(total[...], axis=0, keepdims=True), axis=1, keepdims=True)
    frobenius = jnp.sqrt(sums)
    factor = 0.25 * newton_scale / frobenius
    scale = 1.0 / jnp.sqrt(jnp.sqrt(frobenius / newton_scale))

    eye_big = (
        lax.broadcasted_iota(jnp.int32, (BIG, BIG), 0)
        == lax.broadcasted_iota(jnp.int32, (BIG, BIG), 1)
    ).astype(jnp.float32)

    def big(i):
        return slice(i * BIG, (i + 1) * BIG)

    for i in range(4):
        for j in range(4):
            value = -factor * mat[big(i), big(j)]
            if i == j:
                value += (1.25 - factor * damping) * eye_big
            mat[big(i), big(j)] = value
            f_hi[big(i), big(j)], f_lo[big(i), big(j)] = split(value)

    def triple(a_hi, a_lo, b_hi, b_lo, j):
        rows = slice(0, (j + 1) * BIG)
        return (
            jnp.dot(a_hi[rows, :], b_hi[:, big(j)], preferred_element_type=jnp.float32)
            + jnp.dot(a_hi[rows, :], b_lo[:, big(j)], preferred_element_type=jnp.float32)
            + jnp.dot(a_lo[rows, :], b_hi[:, big(j)], preferred_element_type=jnp.float32)
        )

    def store(hi, lo, i, j, value):
        hi[big(i), big(j)], lo[big(i), big(j)] = split(value)
        if i != j:
            hi[big(j), big(i)], lo[big(j), big(i)] = split(value.T)

    def squared(hi, lo, done):
        for j in range(4):
            cross[:, big(j)] = jnp.dot(
                hi[...], lo[:, big(j)], preferred_element_type=jnp.float32
            )
        for j in range(4):
            value = jnp.dot(
                hi[:(j + 1) * BIG, :], hi[:, big(j)], preferred_element_type=jnp.float32
            )
            for i in range(j + 1):
                done(i, j, value[big(i), :] + (cross[big(i), big(j)] + cross[big(j), big(i)].T))

    def square_done(i, j, part):
        store(q_hi, q_lo, i, j, part)
        store(t_hi, t_lo, i, j, 1.25 * mat[big(i), big(j)] - part)

    squared(f_hi, f_lo, square_done)
    squared(q_hi, q_lo, lambda i, j, part: store(f_hi, f_lo, i, j, part))
    for j in range(4):
        value = triple(f_hi, f_lo, t_hi, t_lo, j)
        for i in range(j + 1):
            part = scale * (1.25 * mat[big(i), big(j)] - value[big(i), :])
            store(q_hi, q_lo, i, j, part)
    copies = []
    for i in range(4):
        out_ref[big(i), :] = jnp.dot(
            q_hi[big(i), :], grad_ref[...], preferred_element_type=jnp.float32
        ) + jnp.dot(q_lo[big(i), :], grad_ref[...], preferred_element_type=jnp.float32)
        copies.append(
            pltpu.make_async_copy(out_ref.at[big(i), :], out_hbm.at[big(i), :], sem_out.at[i])
        )
        copies[-1].start()
    for copy in copies:
        copy.wait()


def local(gradient, stat_old):
    vmem = pl.BlockSpec(memory_space=pltpu.VMEM)
    anywhere = pl.BlockSpec(memory_space=pl.ANY)

    def kept(value):
        return pltpu.with_memory_space_constraint(value, pltpu.VMEM)

    packed = tuple(pltpu.VMEM((4, rows, SUB), jnp.float32) for rows in PARTS)
    blocks = pltpu.VMEM((5, BIG, BIG), jnp.float32)
    limit = pltpu.CompilerParams(vmem_limit_bytes=8 << 20)
    *for_other, grad_kept, old_kept = pl.pallas_call(
        load_kernel,
        out_shape=packed
        + tuple(pltpu.VMEM(value.shape, value.dtype) for value in (gradient, stat_old)),
        in_specs=[anywhere] * 2,
        out_specs=(vmem,) * 4,
        scratch_shapes=[blocks, pltpu.SemaphoreType.DMA((2,))],
        compiler_params=limit,
        name="gram_other",
    )(*(pltpu.with_memory_space_constraint(value, pltpu.HBM) for value in (gradient, stat_old)))
    grad_kept = kept(grad_kept)

    def move(value, first=0, second=0, other=0):
        return lax.ppermute(value, PLANE, pairs(first, second, other))

    arrived = [move(value, other=1) for value in for_other]
    own = pl.pallas_call(
        lambda *refs: gram_kernel(0, *refs),
        out_shape=packed,
        in_specs=[vmem] * 2,
        out_specs=(vmem,) * 2,
        scratch_shapes=[blocks],
        compiler_params=limit,
        name="gram_own",
    )(grad_kept, kept(old_kept))

    mine, theirs = [], []
    for part in range(2):
        sums = [own[part][k] + arrived[part][k] for k in range(4)]
        for k in (2, 1, 3):
            sums[k] = move(sums[k], first=k)
        chunk = (sums[0] + sums[1]) + (sums[2] + sums[3])
        others = [move(chunk, second=k) for k in (2, 1, 3)]
        chunk = (chunk + others[0]) + (others[1] + others[2])
        gathered = [chunk] + [move(chunk, first=k) for k in (2, 1, 3)]
        mine.append(gathered)
        theirs.append([move(value, other=1) for value in gathered])
    chunks = mine[0] + theirs[0] + mine[1] + theirs[1]

    square = (ORDER, ORDER)
    return pl.pallas_call(
        root_kernel,
        out_shape=(
            jax.ShapeDtypeStruct(gradient.shape, jnp.float32),
            jax.ShapeDtypeStruct(stat_old.shape, jnp.float32),
        ),
        in_specs=[vmem] * 17,
        out_specs=(anywhere, vmem),
        scratch_shapes=[pltpu.VMEM(square, jnp.float32)] * 2
        + [pltpu.VMEM(square, jnp.bfloat16)] * 6
        + [
            pltpu.VMEM((SUB, SUB), jnp.float32),
            pltpu.VMEM(gradient.shape, jnp.float32),
            pltpu.SemaphoreType.DMA((4,)),
        ],
        compiler_params=pltpu.CompilerParams(vmem_limit_bytes=44 << 20),
        name="root",
    )(*map(kept, chunks), grad_kept)


def solution(mesh):
    fine = Mesh(mesh.devices.reshape(8, 2, 4, 2, 2), ("row",) + PLANE)
    placed = (P("row", PLANE), P(("row",) + PLANE, None))
    return jax.shard_map(
        local, mesh=fine, in_specs=placed, out_specs=placed, check_vma=False
    )
```

```python
import jax
import jax.numpy as jnp
from jax import lax
from jax.experimental import pallas as pl
from jax.experimental.pallas import tpu as pltpu
from jax.sharding import Mesh, PartitionSpec as P

COLS = 28672
ORDER = 1024
BIG = 256
SUB = 128
PARTS = (BIG, BIG + 8)

damping = 0.001
stat_decay = 0.9
newton_scale = 2.5
weight_new = (1.0 - stat_decay) / COLS

ORIGINS = (0, 2, 1, 3)
PLANE = ("xh", "y", "core", "xl")


def pairs(first, second, other):
    found = []
    for x in range(4):
        for y in range(4):
            for core in range(2):
                dx, dy = (second, first) if core else (first, second)
                ends = []
                for u, v, w in ((x, y, core), ((x + dx) % 4, (y + dy) % 4, core ^ other)):
                    ends.append(((u // 2 * 4 + v) * 2 + w) * 2 + u % 2)
                found.append(tuple(ends))
    return found


def position():
    places = lax.axis_index("xh") * 2 + lax.axis_index("xl"), lax.axis_index("y")
    core = lax.axis_index("core")
    panel = (
        lax.axis_index("xh") * 16 + lax.axis_index("y") * 4 + core * 2 + lax.axis_index("xl")
    )
    return places, core, panel


OFF_BLOCKS = (((0, 1), (0, 2), (0, 3)), ((1, 2), (1, 3), (2, 3)))


def off_block(half, which):
    row = jnp.where(half == 0, 0, jnp.where(which == 3, 2, 1))
    col = jnp.where(half == 0, which, jnp.where(which == 1, 2, 3))
    return row, col


def sub_masks():
    rows = lax.broadcasted_iota(jnp.int32, (SUB, SUB), 0)
    cols = lax.broadcasted_iota(jnp.int32, (SUB, SUB), 1)
    return rows <= cols, rows == cols


def load_kernel(grad_hbm, old_hbm, left_ref, right_ref, grad_ref, old_ref, blocks, sems):
    copies = [
        pltpu.make_async_copy(grad_hbm, grad_ref, sems.at[0]),
        pltpu.make_async_copy(old_hbm, old_ref, sems.at[1]),
    ]
    for copy in copies:
        copy.start()
    for copy in copies:
        copy.wait()
    gram_kernel(1, grad_ref, old_ref, left_ref, right_ref, blocks)


def gram_kernel(flip, grad_ref, old_ref, left_ref, right_ref, blocks):
    places, core, panel = position()
    half = jnp.bitwise_xor(core, flip)
    place = jnp.where(half == 0, places[0], places[1])
    old_big = panel // 8
    old_row = pl.multiple_of((panel % 8) * 32, 32)
    upper, diagonal = sub_masks()

    def big(index):
        return pl.ds(pl.multiple_of(index * BIG, BIG), BIG)

    which = [(place + k) % 4 for k in range(4)]
    where = []
    for k in range(4):
        row, col = off_block(half, which[k])
        where.append(tuple(jnp.where(which[k] == 0, 2 * half, v) for v in (row, col)))
    where.append((2 * half + 1, 2 * half + 1))
    for n, (row, col) in enumerate(where):
        blocks[n] = weight_new * lax.dot_general(
            grad_ref[big(row), :],
            grad_ref[big(col), :],
            (((1,), (1,)), ((), ())),
            preferred_element_type=jnp.float32,
        )
    for n, (row, col) in enumerate(where):

        @pl.when(old_big == row)
        def _():
            blocks[n, pl.ds(old_row, 32), :] += stat_decay * old_ref[:, big(col)]

    for k in range(4):

        @pl.when(which[k] == 0)
        def _():
            extra = []
            for n, ref in ((k, left_ref), (4, right_ref)):
                second = blocks[n, SUB:, SUB:]
                ref[k, :SUB, :] = blocks[n, :SUB, SUB:]
                ref[k, SUB:BIG, :] = jnp.where(upper, blocks[n, :SUB, :SUB], second)
                extra.append(jnp.sum(jnp.where(diagonal, second, 0.0), axis=0, keepdims=True))
            right_ref[k, BIG:, :] = jnp.concatenate(
                extra + [jnp.zeros((6, SUB), jnp.float32)], axis=0
            )

        @pl.when(which[k] != 0)
        def _():
            left_ref[k] = blocks[k, :, :SUB]
            right_ref[k, :BIG, :] = blocks[k, :, SUB:]
            right_ref[k, BIG:, :] = jnp.zeros((8, SUB), jnp.float32)


def split(value):
    high = value.astype(jnp.bfloat16)
    return high, (value - high.astype(jnp.float32)).astype(jnp.bfloat16)


def big(i):
    return slice(i * BIG, (i + 1) * BIG)


def sub(i):
    return slice(i * SUB, (i + 1) * SUB)


def root_kernel(*refs):
    grad_ref, out_hbm, stat_ref = refs[16:19]
    sorted_ref, mat, cross, f_hi, f_lo, q_hi, q_lo, t_hi, t_lo, out_ref, sem_out = refs[19:]
    places, core, panel = position()
    upper, diagonal = sub_masks()

    for n in range(8):
        half = jnp.bitwise_xor(core, n // 4)
        which = (jnp.where(half == 0, places[0], places[1]) + 4 - ORIGINS[n % 4]) % 4
        chunk = half * 4 + which
        sorted_ref[chunk, :BIG, :] = refs[n][...]
        sorted_ref[chunk, BIG:, :] = refs[8 + n][...]

    total = jnp.zeros((8, SUB), jnp.float32)

    def folded(value):
        return jnp.sum(value.reshape(-1, 8, SUB), axis=0)

    for half in range(2):
        for d in range(2):
            start = d * BIG
            value = sorted_ref[half * 4, start:start + SUB, :]
            both = sorted_ref[half * 4, start + SUB:start + BIG, :]
            total += folded(2.0 * value * value)
            damped = both + damping
            total += folded(jnp.where(diagonal, damped * damped, 2.0 * both * both))
            line = sorted_ref[half * 4, 2 * BIG + d:2 * BIG + d + 1, :] + damping
            total += jnp.where(
                lax.broadcasted_iota(jnp.int32, (8, SUB), 0) == 0, line * line, 0.0
            )
        for which in range(1, 4):
            value = sorted_ref[half * 4 + which, :2 * BIG, :]
            total += folded(2.0 * value * value)
    sums = jnp.sum(jnp.sum(total, axis=0, keepdims=True), axis=1, keepdims=True)
    frobenius = jnp.sqrt(sums)
    factor = 0.25 * newton_scale / frobenius
    scale = 1.0 / jnp.sqrt(jnp.sqrt(frobenius / newton_scale))
    shift = 1.25 - factor * damping

    def put(rows, cols, value, on_diagonal=False, keep=True):
        cross[rows, cols] = value
        first = -factor * value
        if on_diagonal:
            first += jnp.where(diagonal, shift, 0.0)
        if keep:
            mat[rows, cols] = first
        f_hi[rows, cols], f_lo[rows, cols] = split(first)

    for half in range(2):
        for d in range(2):
            at = 2 * half + d
            start = d * BIG
            value = sorted_ref[half * 4, start:start + SUB, :]
            put(sub(2 * at), sub(2 * at + 1), value)
            put(sub(2 * at + 1), sub(2 * at), value.T)
            both = sorted_ref[half * 4, start + SUB:start + BIG, :]
            flipped = both.T
            line = sorted_ref[half * 4, 2 * BIG + d:2 * BIG + d + 1, :]
            put(sub(2 * at), sub(2 * at), jnp.where(upper, both, flipped), True)
            second = jnp.where(
                diagonal,
                jnp.broadcast_to(line, (SUB, SUB)),
                jnp.where(upper, flipped, both),
            )
            put(sub(2 * at + 1), sub(2 * at + 1), second, True)
        for which in range(1, 4):
            row, col = OFF_BLOCKS[half][which - 1]
            for part in range(2):
                value = sorted_ref[half * 4 + which, part * BIG:(part + 1) * BIG, :]
                put(big(row), sub(2 * col + part), value)
                put(sub(2 * col + part), big(row), value.T, keep=False)
    stat_ref[...] = cross[pl.ds(pl.multiple_of(panel * 32, 32), 32), :]

    def triple(a_hi, a_lo, b_hi, b_lo, j):
        rows = slice(0, (j + 1) * BIG)
        return (
            jnp.dot(a_hi[rows, :], b_hi[:, big(j)], preferred_element_type=jnp.float32)
            + jnp.dot(a_hi[rows, :], b_lo[:, big(j)], preferred_element_type=jnp.float32)
            + jnp.dot(a_lo[rows, :], b_hi[:, big(j)], preferred_element_type=jnp.float32)
        )

    def store(hi, lo, i, j, value):
        hi[big(i), big(j)], lo[big(i), big(j)] = split(value)
        if i != j:
            hi[big(j), big(i)], lo[big(j), big(i)] = split(value.T)

    def squared(hi, lo, done):
        for j in range(4):
            cross[:, big(j)] = jnp.dot(
                hi[...], lo[:, big(j)], preferred_element_type=jnp.float32
            )
        for j in range(4):
            value = jnp.dot(
                hi[:(j + 1) * BIG, :], hi[:, big(j)], preferred_element_type=jnp.float32
            )
            for i in range(j + 1):
                done(i, j, value[big(i), :] + (cross[big(i), big(j)] + cross[big(j), big(i)].T))

    def square_done(i, j, part):
        store(q_hi, q_lo, i, j, part)
        store(t_hi, t_lo, i, j, 1.25 * mat[big(i), big(j)] - part)

    squared(f_hi, f_lo, square_done)
    squared(q_hi, q_lo, lambda i, j, part: store(f_hi, f_lo, i, j, part))
    for j in range(4):
        value = triple(f_hi, f_lo, t_hi, t_lo, j)
        for i in range(j + 1):
            part = scale * (1.25 * mat[big(i), big(j)] - value[big(i), :])
            store(q_hi, q_lo, i, j, part)
    copies = []
    for n in range(4):
        cols = slice(n * BIG, min((n + 1) * BIG, grad_ref.shape[1]))
        out_ref[:, cols] = jnp.dot(
            q_hi[...], grad_ref[:, cols], preferred_element_type=jnp.float32
        ) + jnp.dot(q_lo[...], grad_ref[:, cols], preferred_element_type=jnp.float32)
        copies.append(
            pltpu.make_async_copy(out_ref.at[:, cols], out_hbm.at[:, cols], sem_out.at[n])
        )
        copies[-1].start()
    for copy in copies:
        copy.wait()


def local(gradient, stat_old):
    vmem = pl.BlockSpec(memory_space=pltpu.VMEM)
    anywhere = pl.BlockSpec(memory_space=pl.ANY)

    def kept(value):
        return pltpu.with_memory_space_constraint(value, pltpu.VMEM)

    packed = tuple(pltpu.VMEM((4, rows, SUB), jnp.float32) for rows in PARTS)
    blocks = pltpu.VMEM((5, BIG, BIG), jnp.float32)
    limit = pltpu.CompilerParams(vmem_limit_bytes=8 << 20)
    *for_other, grad_kept, old_kept = pl.pallas_call(
        load_kernel,
        out_shape=packed
        + tuple(pltpu.VMEM(value.shape, value.dtype) for value in (gradient, stat_old)),
        in_specs=[anywhere] * 2,
        out_specs=(vmem,) * 4,
        scratch_shapes=[blocks, pltpu.SemaphoreType.DMA((2,))],
        compiler_params=limit,
        name="gram_other",
    )(*(pltpu.with_memory_space_constraint(value, pltpu.HBM) for value in (gradient, stat_old)))
    grad_kept = kept(grad_kept)

    def move(value, first=0, second=0, other=0):
        return lax.ppermute(value, PLANE, pairs(first, second, other))

    arrived = [move(value, other=1) for value in for_other]
    own = pl.pallas_call(
        lambda *refs: gram_kernel(0, *refs),
        out_shape=packed,
        in_specs=[vmem] * 2,
        out_specs=(vmem,) * 2,
        scratch_shapes=[blocks],
        compiler_params=limit,
        name="gram_own",
    )(grad_kept, kept(old_kept))

    mine, theirs = [], []
    for part in range(2):
        sums = [own[part][k] + arrived[part][k] for k in range(4)]
        for k in (2, 1, 3):
            sums[k] = move(sums[k], first=k)
        chunk = (sums[0] + sums[1]) + (sums[2] + sums[3])
        others = [move(chunk, second=k) for k in (2, 1, 3)]
        chunk = (chunk + others[0]) + (others[1] + others[2])
        gathered = [chunk] + [move(chunk, first=k) for k in (2, 1, 3)]
        mine.append(gathered)
        theirs.append([move(value, other=1) for value in gathered])
    chunks = mine[0] + theirs[0] + mine[1] + theirs[1]

    square = (ORDER, ORDER)
    return pl.pallas_call(
        root_kernel,
        out_shape=(
            jax.ShapeDtypeStruct(gradient.shape, jnp.float32),
            jax.ShapeDtypeStruct(stat_old.shape, jnp.float32),
        ),
        in_specs=[vmem] * 17,
        out_specs=(anywhere, vmem),
        scratch_shapes=[pltpu.VMEM((8, sum(PARTS), SUB), jnp.float32)]
        + [pltpu.VMEM(square, jnp.float32)] * 2
        + [pltpu.VMEM(square, jnp.bfloat16)] * 6
        + [
            pltpu.VMEM(gradient.shape, jnp.float32),
            pltpu.SemaphoreType.DMA((4,)),
        ],
        compiler_params=pltpu.CompilerParams(vmem_limit_bytes=44 << 20),
        name="root",
    )(*map(kept, chunks), grad_kept)


def solution(mesh):
    fine = Mesh(mesh.devices.reshape(8, 2, 4, 2, 2), ("row",) + PLANE)
    placed = (P("row", PLANE), P(("row",) + PLANE, None))
    return jax.shard_map(
        local, mesh=fine, in_specs=placed, out_specs=placed, check_vma=False
    )
```

```python
import jax
import jax.numpy as jnp
from jax import lax
from jax.experimental import pallas as pl
from jax.experimental.pallas import tpu as pltpu
from jax.sharding import Mesh, PartitionSpec as P

COLS = 28672
ORDER = 1024
BIG = 256
SUB = 128
PARTS = (BIG, BIG + 8)

damping = 0.001
stat_decay = 0.9
newton_scale = 2.5
weight_new = (1.0 - stat_decay) / COLS

ORIGINS = (0, 2, 1, 3)
PLANE = ("xh", "y", "core", "xl")


def shift(by):
    return lambda place: (place + by) % 4


def neighbour(step):
    return lambda place: place ^ 1 if step == 0 else 3 - place


def pairs(first=None, second=None, other=0):
    same = shift(0)
    found = []
    for x in range(4):
        for y in range(4):
            for core in range(2):
                along_x, along_y = (second, first) if core else (first, second)
                ends = []
                for u, v, w in ((x, y, core), ((along_x or same)(x), (along_y or same)(y), core ^ other)):
                    ends.append(((u // 2 * 4 + v) * 2 + w) * 2 + u % 2)
                found.append(tuple(ends))
    return found


def position():
    places = lax.axis_index("xh") * 2 + lax.axis_index("xl"), lax.axis_index("y")
    core = lax.axis_index("core")
    panel = (
        lax.axis_index("xh") * 16 + lax.axis_index("y") * 4 + core * 2 + lax.axis_index("xl")
    )
    return places, core, panel


OFF_BLOCKS = (((0, 1), (0, 2), (0, 3)), ((1, 2), (1, 3), (2, 3)))


def off_block(half, which):
    row = jnp.where(half == 0, 0, jnp.where(which == 3, 2, 1))
    col = jnp.where(half == 0, which, jnp.where(which == 1, 2, 3))
    return row, col


def sub_masks():
    rows = lax.broadcasted_iota(jnp.int32, (SUB, SUB), 0)
    cols = lax.broadcasted_iota(jnp.int32, (SUB, SUB), 1)
    return rows <= cols, rows == cols


def load_kernel(grad_hbm, old_hbm, left_ref, right_ref, grad_ref, old_ref, blocks, sems):
    copies = [
        pltpu.make_async_copy(grad_hbm, grad_ref, sems.at[0]),
        pltpu.make_async_copy(old_hbm, old_ref, sems.at[1]),
    ]
    for copy in copies:
        copy.start()
    for copy in copies:
        copy.wait()
    gram_kernel(1, grad_ref, old_ref, left_ref, right_ref, blocks)


def gram_kernel(flip, grad_ref, old_ref, left_ref, right_ref, blocks):
    places, core, panel = position()
    half = jnp.bitwise_xor(core, flip)
    place = jnp.where(half == 0, places[0], places[1])
    old_big = panel // 8
    old_row = pl.multiple_of((panel % 8) * 32, 32)
    upper, diagonal = sub_masks()

    def big(index):
        return pl.ds(pl.multiple_of(index * BIG, BIG), BIG)

    which = [(place + k) % 4 for k in range(4)]
    where = []
    for k in range(4):
        row, col = off_block(half, which[k])
        where.append(tuple(jnp.where(which[k] == 0, 2 * half, v) for v in (row, col)))
    where.append((2 * half + 1, 2 * half + 1))
    for n, (row, col) in enumerate(where):
        blocks[n] = weight_new * lax.dot_general(
            grad_ref[big(row), :],
            grad_ref[big(col), :],
            (((1,), (1,)), ((), ())),
            preferred_element_type=jnp.float32,
        )
    for n, (row, col) in enumerate(where):

        @pl.when(old_big == row)
        def _():
            blocks[n, pl.ds(old_row, 32), :] += stat_decay * old_ref[:, big(col)]

    for k in range(4):

        @pl.when(which[k] == 0)
        def _():
            extra = []
            for n, ref in ((k, left_ref), (4, right_ref)):
                second = blocks[n, SUB:, SUB:]
                ref[k, :SUB, :] = blocks[n, :SUB, SUB:]
                ref[k, SUB:BIG, :] = jnp.where(upper, blocks[n, :SUB, :SUB], second)
                extra.append(jnp.sum(jnp.where(diagonal, second, 0.0), axis=0, keepdims=True))
            right_ref[k, BIG:, :] = jnp.concatenate(
                extra + [jnp.zeros((6, SUB), jnp.float32)], axis=0
            )

        @pl.when(which[k] != 0)
        def _():
            left_ref[k] = blocks[k, :, :SUB]
            right_ref[k, :BIG, :] = blocks[k, :, SUB:]
            right_ref[k, BIG:, :] = jnp.zeros((8, SUB), jnp.float32)


def split(value):
    high = value.astype(jnp.bfloat16)
    return high, (value - high.astype(jnp.float32)).astype(jnp.bfloat16)


def big(i):
    return slice(i * BIG, (i + 1) * BIG)


def sub(i):
    return slice(i * SUB, (i + 1) * SUB)


def root_kernel(*refs):
    grad_ref, out_hbm, stat_ref = refs[16:19]
    sorted_ref, mat, cross, f_hi, f_lo, q_hi, q_lo, t_hi, t_lo, out_ref, sem_out = refs[19:]
    places, core, panel = position()
    upper, diagonal = sub_masks()

    for n in range(8):
        half = jnp.bitwise_xor(core, n // 4)
        which = (jnp.where(half == 0, places[0], places[1]) + 4 - ORIGINS[n % 4]) % 4
        chunk = half * 4 + which
        sorted_ref[chunk, :BIG, :] = refs[n][...]
        sorted_ref[chunk, BIG:, :] = refs[8 + n][...]

    total = jnp.zeros((8, SUB), jnp.float32)

    def folded(value):
        return jnp.sum(value.reshape(-1, 8, SUB), axis=0)

    for half in range(2):
        for d in range(2):
            start = d * BIG
            value = sorted_ref[half * 4, start:start + SUB, :]
            both = sorted_ref[half * 4, start + SUB:start + BIG, :]
            total += folded(2.0 * value * value)
            damped = both + damping
            total += folded(jnp.where(diagonal, damped * damped, 2.0 * both * both))
            line = sorted_ref[half * 4, 2 * BIG + d:2 * BIG + d + 1, :] + damping
            total += jnp.where(
                lax.broadcasted_iota(jnp.int32, (8, SUB), 0) == 0, line * line, 0.0
            )
        for which in range(1, 4):
            value = sorted_ref[half * 4 + which, :2 * BIG, :]
            total += folded(2.0 * value * value)
    sums = jnp.sum(jnp.sum(total, axis=0, keepdims=True), axis=1, keepdims=True)
    frobenius = jnp.sqrt(sums)
    factor = 0.25 * newton_scale / frobenius
    scale = 1.0 / jnp.sqrt(jnp.sqrt(frobenius / newton_scale))
    shift = 1.25 - factor * damping

    def put(rows, cols, value, on_diagonal=False, keep=True):
        cross[rows, cols] = value
        first = -factor * value
        if on_diagonal:
            first += jnp.where(diagonal, shift, 0.0)
        if keep:
            mat[rows, cols] = first
        f_hi[rows, cols], f_lo[rows, cols] = split(first)

    for half in range(2):
        for d in range(2):
            at = 2 * half + d
            start = d * BIG
            value = sorted_ref[half * 4, start:start + SUB, :]
            put(sub(2 * at), sub(2 * at + 1), value)
            put(sub(2 * at + 1), sub(2 * at), value.T)
            both = sorted_ref[half * 4, start + SUB:start + BIG, :]
            flipped = both.T
            line = sorted_ref[half * 4, 2 * BIG + d:2 * BIG + d + 1, :]
            put(sub(2 * at), sub(2 * at), jnp.where(upper, both, flipped), True)
            second = jnp.where(
                diagonal,
                jnp.broadcast_to(line, (SUB, SUB)),
                jnp.where(upper, flipped, both),
            )
            put(sub(2 * at + 1), sub(2 * at + 1), second, True)
        for which in range(1, 4):
            row, col = OFF_BLOCKS[half][which - 1]
            for part in range(2):
                value = sorted_ref[half * 4 + which, part * BIG:(part + 1) * BIG, :]
                put(big(row), sub(2 * col + part), value)
                put(sub(2 * col + part), big(row), value.T, keep=False)
    stat_ref[...] = cross[pl.ds(pl.multiple_of(panel * 32, 32), 32), :]

    def triple(a_hi, a_lo, b_hi, b_lo, j):
        rows = slice(0, (j + 1) * BIG)
        return (
            jnp.dot(a_hi[rows, :], b_hi[:, big(j)], preferred_element_type=jnp.float32)
            + jnp.dot(a_hi[rows, :], b_lo[:, big(j)], preferred_element_type=jnp.float32)
            + jnp.dot(a_lo[rows, :], b_hi[:, big(j)], preferred_element_type=jnp.float32)
        )

    def store(hi, lo, i, j, value):
        hi[big(i), big(j)], lo[big(i), big(j)] = split(value)
        if i != j:
            hi[big(j), big(i)], lo[big(j), big(i)] = split(value.T)

    def squared(hi, lo, done):
        for j in range(4):
            cross[:, big(j)] = jnp.dot(
                hi[...], lo[:, big(j)], preferred_element_type=jnp.float32
            )
        for j in range(4):
            value = jnp.dot(
                hi[:(j + 1) * BIG, :], hi[:, big(j)], preferred_element_type=jnp.float32
            )
            for i in range(j + 1):
                done(i, j, value[big(i), :] + (cross[big(i), big(j)] + cross[big(j), big(i)].T))

    def square_done(i, j, part):
        store(q_hi, q_lo, i, j, part)
        store(t_hi, t_lo, i, j, 1.25 * mat[big(i), big(j)] - part)

    squared(f_hi, f_lo, square_done)
    squared(q_hi, q_lo, lambda i, j, part: store(f_hi, f_lo, i, j, part))
    for j in range(4):
        value = triple(f_hi, f_lo, t_hi, t_lo, j)
        for i in range(j + 1):
            part = scale * (1.25 * mat[big(i), big(j)] - value[big(i), :])
            store(q_hi, q_lo, i, j, part)
    copies = []
    for n in range(4):
        cols = slice(n * BIG, min((n + 1) * BIG, grad_ref.shape[1]))
        out_ref[:, cols] = jnp.dot(
            q_hi[...], grad_ref[:, cols], preferred_element_type=jnp.float32
        ) + jnp.dot(q_lo[...], grad_ref[:, cols], preferred_element_type=jnp.float32)
        copies.append(
            pltpu.make_async_copy(out_ref.at[:, cols], out_hbm.at[:, cols], sem_out.at[n])
        )
        copies[-1].start()
    for copy in copies:
        copy.wait()


def local(gradient, stat_old):
    vmem = pl.BlockSpec(memory_space=pltpu.VMEM)
    anywhere = pl.BlockSpec(memory_space=pl.ANY)

    def kept(value):
        return pltpu.with_memory_space_constraint(value, pltpu.VMEM)

    packed = tuple(pltpu.VMEM((4, rows, SUB), jnp.float32) for rows in PARTS)
    blocks = pltpu.VMEM((5, BIG, BIG), jnp.float32)
    limit = pltpu.CompilerParams(vmem_limit_bytes=8 << 20)
    *for_other, grad_kept, old_kept = pl.pallas_call(
        load_kernel,
        out_shape=packed
        + tuple(pltpu.VMEM(value.shape, value.dtype) for value in (gradient, stat_old)),
        in_specs=[anywhere] * 2,
        out_specs=(vmem,) * 4,
        scratch_shapes=[blocks, pltpu.SemaphoreType.DMA((2,))],
        compiler_params=limit,
        name="gram_other",
    )(*(pltpu.with_memory_space_constraint(value, pltpu.HBM) for value in (gradient, stat_old)))
    grad_kept = kept(grad_kept)

    def move(value, **where):
        return lax.ppermute(value, PLANE, pairs(**where))

    arrived = [move(value, other=1) for value in for_other]
    own = pl.pallas_call(
        lambda *refs: gram_kernel(0, *refs),
        out_shape=packed,
        in_specs=[vmem] * 2,
        out_specs=(vmem,) * 2,
        scratch_shapes=[blocks],
        compiler_params=limit,
        name="gram_own",
    )(grad_kept, kept(old_kept))

    mine, theirs = [], []
    for part in range(2):
        sums = [own[part][k] + arrived[part][k] for k in range(4)]
        for k in (2, 1, 3):
            sums[k] = move(sums[k], first=shift(k))
        chunk = (sums[0] + sums[1]) + (sums[2] + sums[3])
        for step in range(2):
            chunk = chunk + move(chunk, second=neighbour(step ^ part))
        gathered = [chunk] + [move(chunk, first=shift(k)) for k in (2, 1, 3)]
        mine.append(gathered)
        theirs.append([move(value, other=1) for value in gathered])
    chunks = mine[0] + theirs[0] + mine[1] + theirs[1]

    square = (ORDER, ORDER)
    return pl.pallas_call(
        root_kernel,
        out_shape=(
            jax.ShapeDtypeStruct(gradient.shape, jnp.float32),
            jax.ShapeDtypeStruct(stat_old.shape, jnp.float32),
        ),
        in_specs=[vmem] * 17,
        out_specs=(anywhere, vmem),
        scratch_shapes=[pltpu.VMEM((8, sum(PARTS), SUB), jnp.float32)]
        + [pltpu.VMEM(square, jnp.float32)] * 2
        + [pltpu.VMEM(square, jnp.bfloat16)] * 6
        + [
            pltpu.VMEM(gradient.shape, jnp.float32),
            pltpu.SemaphoreType.DMA((4,)),
        ],
        compiler_params=pltpu.CompilerParams(vmem_limit_bytes=44 << 20),
        name="root",
    )(*map(kept, chunks), grad_kept)


def solution(mesh):
    fine = Mesh(mesh.devices.reshape(8, 2, 4, 2, 2), ("row",) + PLANE)
    placed = (P("row", PLANE), P(("row",) + PLANE, None))
    return jax.shard_map(
        local, mesh=fine, in_specs=placed, out_specs=placed, check_vma=False
    )
```

```python
import jax
import jax.numpy as jnp
from jax import lax
from jax.experimental import pallas as pl
from jax.experimental.pallas import tpu as pltpu
from jax.sharding import Mesh, PartitionSpec as P

COLS = 28672
ORDER = 1024
BIG = 256
SUB = 128
PARTS = (BIG, BIG + 8)

damping = 0.001
stat_decay = 0.9
newton_scale = 2.5
weight_new = (1.0 - stat_decay) / COLS

ORIGINS = (0, 2, 1, 3)
PLANE = ("xh", "y", "core", "xl")


def pairs(first, second, other):
    found = []
    for x in range(4):
        for y in range(4):
            for core in range(2):
                dx, dy = (second, first) if core else (first, second)
                ends = []
                for u, v, w in ((x, y, core), ((x + dx) % 4, (y + dy) % 4, core ^ other)):
                    ends.append(((u // 2 * 4 + v) * 2 + w) * 2 + u % 2)
                found.append(tuple(ends))
    return found


def position():
    places = lax.axis_index("xh") * 2 + lax.axis_index("xl"), lax.axis_index("y")
    core = lax.axis_index("core")
    panel = (
        lax.axis_index("xh") * 16 + lax.axis_index("y") * 4 + core * 2 + lax.axis_index("xl")
    )
    return places, core, panel


OFF_BLOCKS = (((0, 1), (0, 2), (0, 3)), ((1, 2), (1, 3), (2, 3)))


def off_block(half, which):
    row = jnp.where(half == 0, 0, jnp.where(which == 3, 2, 1))
    col = jnp.where(half == 0, which, jnp.where(which == 1, 2, 3))
    return row, col


def sub_masks():
    rows = lax.broadcasted_iota(jnp.int32, (SUB, SUB), 0)
    cols = lax.broadcasted_iota(jnp.int32, (SUB, SUB), 1)
    return rows <= cols, rows == cols


def load_kernel(grad_hbm, old_hbm, left_ref, right_ref, grad_ref, old_ref, blocks, sems):
    copies = [
        pltpu.make_async_copy(grad_hbm, grad_ref, sems.at[0]),
        pltpu.make_async_copy(old_hbm, old_ref, sems.at[1]),
    ]
    for copy in copies:
        copy.start()
    for copy in copies:
        copy.wait()
    gram_kernel(1, grad_ref, old_ref, left_ref, right_ref, blocks)


def gram_kernel(flip, grad_ref, old_ref, left_ref, right_ref, blocks):
    places, core, panel = position()
    half = jnp.bitwise_xor(core, flip)
    place = jnp.where(half == 0, places[0], places[1])
    old_big = panel // 8
    old_row = pl.multiple_of((panel % 8) * 32, 32)
    upper, diagonal = sub_masks()

    def big(index):
        return pl.ds(pl.multiple_of(index * BIG, BIG), BIG)

    which = [(place + k) % 4 for k in range(4)]
    where = []
    for k in range(4):
        row, col = off_block(half, which[k])
        where.append(tuple(jnp.where(which[k] == 0, 2 * half, v) for v in (row, col)))
    where.append((2 * half + 1, 2 * half + 1))
    for n, (row, col) in enumerate(where):
        blocks[n] = weight_new * lax.dot_general(
            grad_ref[big(row), :],
            grad_ref[big(col), :],
            (((1,), (1,)), ((), ())),
            preferred_element_type=jnp.float32,
        )
    for n, (row, col) in enumerate(where):

        @pl.when(old_big == row)
        def _():
            blocks[n, pl.ds(old_row, 32), :] += stat_decay * old_ref[:, big(col)]

    for k in range(4):

        @pl.when(which[k] == 0)
        def _():
            extra = []
            for n, ref in ((k, left_ref), (4, right_ref)):
                second = blocks[n, SUB:, SUB:]
                ref[k, :SUB, :] = blocks[n, :SUB, SUB:]
                ref[k, SUB:BIG, :] = jnp.where(upper, blocks[n, :SUB, :SUB], second)
                extra.append(jnp.sum(jnp.where(diagonal, second, 0.0), axis=0, keepdims=True))
            right_ref[k, BIG:, :] = jnp.concatenate(
                extra + [jnp.zeros((6, SUB), jnp.float32)], axis=0
            )

        @pl.when(which[k] != 0)
        def _():
            left_ref[k] = blocks[k, :, :SUB]
            right_ref[k, :BIG, :] = blocks[k, :, SUB:]
            right_ref[k, BIG:, :] = jnp.zeros((8, SUB), jnp.float32)


def split(value):
    high = value.astype(jnp.bfloat16)
    return high, (value - high.astype(jnp.float32)).astype(jnp.bfloat16)


def big(i):
    return slice(i * BIG, (i + 1) * BIG)


def sub(i):
    return slice(i * SUB, (i + 1) * SUB)


def root_kernel(*refs):
    grad_ref, out_hbm, stat_ref = refs[16:19]
    sorted_ref, mat, cross, work, f_hi, f_lo, q_hi, q_lo, t_hi, t_lo, out_ref, sem_out = refs[19:]
    places, core, panel = position()
    upper, diagonal = sub_masks()

    for n in range(8):
        half = jnp.bitwise_xor(core, n // 4)
        which = (jnp.where(half == 0, places[0], places[1]) + 4 - ORIGINS[n % 4]) % 4
        chunk = half * 4 + which
        sorted_ref[chunk, :BIG, :] = refs[n][...]
        sorted_ref[chunk, BIG:, :] = refs[8 + n][...]

    total = jnp.zeros((8, SUB), jnp.float32)

    def folded(value):
        return jnp.sum(value.reshape(-1, 8, SUB), axis=0)

    for half in range(2):
        for d in range(2):
            start = d * BIG
            value = sorted_ref[half * 4, start:start + SUB, :]
            both = sorted_ref[half * 4, start + SUB:start + BIG, :]
            total += folded(2.0 * value * value)
            damped = both + damping
            total += folded(jnp.where(diagonal, damped * damped, 2.0 * both * both))
            line = sorted_ref[half * 4, 2 * BIG + d:2 * BIG + d + 1, :] + damping
            total += jnp.where(
                lax.broadcasted_iota(jnp.int32, (8, SUB), 0) == 0, line * line, 0.0
            )
        for which in range(1, 4):
            value = sorted_ref[half * 4 + which, :2 * BIG, :]
            total += folded(2.0 * value * value)
    sums = jnp.sum(jnp.sum(total, axis=0, keepdims=True), axis=1, keepdims=True)
    frobenius = jnp.sqrt(sums)
    factor = 0.25 * newton_scale / frobenius
    scale = 1.0 / jnp.sqrt(jnp.sqrt(frobenius / newton_scale))
    shift = 1.25 - factor * damping

    def put(rows, cols, value, on_diagonal=False, keep=True):
        cross[rows, cols] = value
        first = -factor * value
        if on_diagonal:
            first += jnp.where(diagonal, shift, 0.0)
        if keep:
            mat[rows, cols] = first
        f_hi[rows, cols], f_lo[rows, cols] = split(first)

    for half in range(2):
        for d in range(2):
            at = 2 * half + d
            start = d * BIG
            value = sorted_ref[half * 4, start:start + SUB, :]
            put(sub(2 * at), sub(2 * at + 1), value)
            put(sub(2 * at + 1), sub(2 * at), value.T)
            both = sorted_ref[half * 4, start + SUB:start + BIG, :]
            flipped = both.T
            line = sorted_ref[half * 4, 2 * BIG + d:2 * BIG + d + 1, :]
            put(sub(2 * at), sub(2 * at), jnp.where(upper, both, flipped), True)
            second = jnp.where(
                diagonal,
                jnp.broadcast_to(line, (SUB, SUB)),
                jnp.where(upper, flipped, both),
            )
            put(sub(2 * at + 1), sub(2 * at + 1), second, True)
        for which in range(1, 4):
            row, col = OFF_BLOCKS[half][which - 1]
            for part in range(2):
                value = sorted_ref[half * 4 + which, part * BIG:(part + 1) * BIG, :]
                put(big(row), sub(2 * col + part), value)
                put(sub(2 * col + part), big(row), value.T, keep=False)
    stat_ref[...] = cross[pl.ds(pl.multiple_of(panel * 32, 32), 32), :]

    def dots(terms, rows, cols, done):
        middle = (rows.start + rows.stop) // 2
        for part in (slice(rows.start, middle), slice(middle, rows.stop)):
            done(
                part,
                sum(
                    jnp.dot(a[part, :], b[:, cols], preferred_element_type=jnp.float32)
                    for a, b in terms
                ),
            )

    def store(hi, lo, i, j, value):
        hi[big(i), big(j)], lo[big(i), big(j)] = split(value)
        if i != j:
            hi[big(j), big(i)], lo[big(j), big(i)] = split(value.T)

    def keep(ref, cols):
        def done(rows, value):
            ref[rows, cols] = value
        return done

    def squared(hi, lo, done):
        for j in range(4):
            dots([(hi, lo)], slice(0, ORDER), big(j), keep(cross, big(j)))
        for j in range(4):
            dots([(hi, hi)], slice(0, (j + 1) * BIG), big(j), keep(work, big(j)))
            for i in range(j + 1):
                value = work[big(i), big(j)]
                done(i, j, value + (cross[big(i), big(j)] + cross[big(j), big(i)].T))

    def square_done(i, j, part):
        store(q_hi, q_lo, i, j, part)
        store(t_hi, t_lo, i, j, 1.25 * mat[big(i), big(j)] - part)

    squared(f_hi, f_lo, square_done)
    squared(q_hi, q_lo, lambda i, j, part: store(f_hi, f_lo, i, j, part))
    for j in range(4):
        terms = [(f_hi, t_hi), (f_hi, t_lo), (f_lo, t_hi)]
        dots(terms, slice(0, (j + 1) * BIG), big(j), keep(work, big(j)))
        for i in range(j + 1):
            part = scale * (1.25 * mat[big(i), big(j)] - work[big(i), big(j)])
            store(q_hi, q_lo, i, j, part)
    copies = []
    for n in range(4):
        cols = slice(n * BIG, min((n + 1) * BIG, grad_ref.shape[1]))
        dots([(q_hi, grad_ref), (q_lo, grad_ref)], slice(0, ORDER), cols, keep(out_ref, cols))
        copies.append(
            pltpu.make_async_copy(out_ref.at[:, cols], out_hbm.at[:, cols], sem_out.at[n])
        )
        copies[-1].start()
    for copy in copies:
        copy.wait()


def local(gradient, stat_old):
    vmem = pl.BlockSpec(memory_space=pltpu.VMEM)
    anywhere = pl.BlockSpec(memory_space=pl.ANY)

    def kept(value):
        return pltpu.with_memory_space_constraint(value, pltpu.VMEM)

    packed = tuple(pltpu.VMEM((4, rows, SUB), jnp.float32) for rows in PARTS)
    blocks = pltpu.VMEM((5, BIG, BIG), jnp.float32)
    limit = pltpu.CompilerParams(vmem_limit_bytes=8 << 20)
    *for_other, grad_kept, old_kept = pl.pallas_call(
        load_kernel,
        out_shape=packed
        + tuple(pltpu.VMEM(value.shape, value.dtype) for value in (gradient, stat_old)),
        in_specs=[anywhere] * 2,
        out_specs=(vmem,) * 4,
        scratch_shapes=[blocks, pltpu.SemaphoreType.DMA((2,))],
        compiler_params=limit,
        name="gram_other",
    )(*(pltpu.with_memory_space_constraint(value, pltpu.HBM) for value in (gradient, stat_old)))
    grad_kept = kept(grad_kept)

    def move(value, first=0, second=0, other=0):
        return lax.ppermute(value, PLANE, pairs(first, second, other))

    arrived = [move(value, other=1) for value in for_other]
    own = pl.pallas_call(
        lambda *refs: gram_kernel(0, *refs),
        out_shape=packed,
        in_specs=[vmem] * 2,
        out_specs=(vmem,) * 2,
        scratch_shapes=[blocks],
        compiler_params=limit,
        name="gram_own",
    )(grad_kept, kept(old_kept))

    mine, theirs = [], []
    for part in range(2):
        sums = [own[part][k] + arrived[part][k] for k in range(4)]
        for k in (2, 1, 3):
            sums[k] = move(sums[k], first=k)
        chunk = (sums[0] + sums[1]) + (sums[2] + sums[3])
        others = [move(chunk, second=k) for k in (2, 1, 3)]
        chunk = (chunk + others[0]) + (others[1] + others[2])
        gathered = [chunk] + [move(chunk, first=k) for k in (2, 1, 3)]
        mine.append(gathered)
        theirs.append([move(value, other=1) for value in gathered])
    chunks = mine[0] + theirs[0] + mine[1] + theirs[1]

    square = (ORDER, ORDER)
    return pl.pallas_call(
        root_kernel,
        out_shape=(
            jax.ShapeDtypeStruct(gradient.shape, jnp.float32),
            jax.ShapeDtypeStruct(stat_old.shape, jnp.float32),
        ),
        in_specs=[vmem] * 17,
        out_specs=(anywhere, vmem),
        scratch_shapes=[pltpu.VMEM((8, sum(PARTS), SUB), jnp.float32)]
        + [pltpu.VMEM(square, jnp.float32)] * 3
        + [pltpu.VMEM(square, jnp.bfloat16)] * 6
        + [
            pltpu.VMEM(gradient.shape, jnp.float32),
            pltpu.SemaphoreType.DMA((4,)),
        ],
        compiler_params=pltpu.CompilerParams(vmem_limit_bytes=44 << 20),
        name="root",
    )(*map(kept, chunks), grad_kept)


def solution(mesh):
    fine = Mesh(mesh.devices.reshape(8, 2, 4, 2, 2), ("row",) + PLANE)
    placed = (P("row", PLANE), P(("row",) + PLANE, None))
    return jax.shard_map(
        local, mesh=fine, in_specs=placed, out_specs=placed, check_vma=False
    )
```

```python
import jax
import jax.numpy as jnp
from jax import lax
from jax.experimental import pallas as pl
from jax.experimental.pallas import tpu as pltpu
from jax.sharding import Mesh, PartitionSpec as P

COLS = 28672
ORDER = 1024
BIG = 256
SUB = 128
CHUNK = 2 * BIG + 8
ORDER_SENT = ((2, 1), (3, 0))

damping = 0.001
stat_decay = 0.9
newton_scale = 2.5
weight_new = (1.0 - stat_decay) / COLS

ORIGINS = (0, 2, 1, 3)
PLANE = ("xh", "y", "core", "xl")


def pairs(first, second, other):
    found = []
    for x in range(4):
        for y in range(4):
            for core in range(2):
                dx, dy = (second, first) if core else (first, second)
                ends = []
                for u, v, w in ((x, y, core), ((x + dx) % 4, (y + dy) % 4, core ^ other)):
                    ends.append(((u // 2 * 4 + v) * 2 + w) * 2 + u % 2)
                found.append(tuple(ends))
    return found


def position():
    places = lax.axis_index("xh") * 2 + lax.axis_index("xl"), lax.axis_index("y")
    core = lax.axis_index("core")
    panel = (
        lax.axis_index("xh") * 16 + lax.axis_index("y") * 4 + core * 2 + lax.axis_index("xl")
    )
    return places, core, panel


OFF_BLOCKS = (((0, 1), (0, 2), (0, 3)), ((1, 2), (1, 3), (2, 3)))


def off_block(half, which):
    row = jnp.where(half == 0, 0, jnp.where(which == 3, 2, 1))
    col = jnp.where(half == 0, which, jnp.where(which == 1, 2, 3))
    return row, col


def sub_masks():
    rows = lax.broadcasted_iota(jnp.int32, (SUB, SUB), 0)
    cols = lax.broadcasted_iota(jnp.int32, (SUB, SUB), 1)
    return rows <= cols, rows == cols


def load_kernel(grad_hbm, old_hbm, early_ref, late_ref, grad_ref, old_ref, blocks, sems):
    copies = [
        pltpu.make_async_copy(grad_hbm, grad_ref, sems.at[0]),
        pltpu.make_async_copy(old_hbm, old_ref, sems.at[1]),
    ]
    for copy in copies:
        copy.start()
    for copy in copies:
        copy.wait()
    gram_kernel(1, grad_ref, old_ref, early_ref, late_ref, blocks)


def gram_kernel(flip, grad_ref, old_ref, early_ref, late_ref, blocks):
    places, core, panel = position()
    half = jnp.bitwise_xor(core, flip)
    place = jnp.where(half == 0, places[0], places[1])
    old_big = panel // 8
    old_row = pl.multiple_of((panel % 8) * 32, 32)
    upper, diagonal = sub_masks()

    def big(index):
        return pl.ds(pl.multiple_of(index * BIG, BIG), BIG)

    which = [(place + k) % 4 for k in range(4)]
    where = []
    for k in range(4):
        row, col = off_block(half, which[k])
        where.append(tuple(jnp.where(which[k] == 0, 2 * half, v) for v in (row, col)))
    where.append((2 * half + 1, 2 * half + 1))
    for n, (row, col) in enumerate(where):
        blocks[n] = weight_new * lax.dot_general(
            grad_ref[big(row), :],
            grad_ref[big(col), :],
            (((1,), (1,)), ((), ())),
            preferred_element_type=jnp.float32,
        )
    for n, (row, col) in enumerate(where):

        @pl.when(old_big == row)
        def _():
            blocks[n, pl.ds(old_row, 32), :] += stat_decay * old_ref[:, big(col)]

    for k, ref, slot in (
        (k, ref, slot)
        for ref, order in zip((early_ref, late_ref), ORDER_SENT)
        for slot, k in enumerate(order)
    ):

        @pl.when(which[k] == 0)
        def _():
            extra = []
            for d, n in enumerate((k, 4)):
                start = d * BIG
                second = blocks[n, SUB:, SUB:]
                ref[slot, start:start + SUB, :] = blocks[n, :SUB, SUB:]
                ref[slot, start + SUB:start + BIG, :] = jnp.where(
                    upper, blocks[n, :SUB, :SUB], second
                )
                extra.append(jnp.sum(jnp.where(diagonal, second, 0.0), axis=0, keepdims=True))
            ref[slot, 2 * BIG:, :] = jnp.concatenate(
                extra + [jnp.zeros((6, SUB), jnp.float32)], axis=0
            )

        @pl.when(which[k] != 0)
        def _():
            ref[slot, :BIG, :] = blocks[k, :, :SUB]
            ref[slot, BIG:2 * BIG, :] = blocks[k, :, SUB:]
            ref[slot, 2 * BIG:, :] = jnp.zeros((8, SUB), jnp.float32)


def split(value):
    high = value.astype(jnp.bfloat16)
    return high, (value - high.astype(jnp.float32)).astype(jnp.bfloat16)


def big(i):
    return slice(i * BIG, (i + 1) * BIG)


def sub(i):
    return slice(i * SUB, (i + 1) * SUB)


def root_kernel(*refs):
    grad_ref, out_hbm, stat_ref = refs[8:11]
    sorted_ref, mat, cross, work, f_hi, f_lo, q_hi, q_lo, t_hi, t_lo, out_ref, sem_out = refs[11:]
    places, core, panel = position()
    upper, diagonal = sub_masks()

    for n in range(8):
        half = jnp.bitwise_xor(core, n // 4)
        which = (jnp.where(half == 0, places[0], places[1]) + 4 - ORIGINS[n % 4]) % 4
        chunk = half * 4 + which
        sorted_ref[chunk] = refs[n][...]

    total = jnp.zeros((8, SUB), jnp.float32)

    def folded(value):
        return jnp.sum(value.reshape(-1, 8, SUB), axis=0)

    for half in range(2):
        for d in range(2):
            start = d * BIG
            value = sorted_ref[half * 4, start:start + SUB, :]
            both = sorted_ref[half * 4, start + SUB:start + BIG, :]
            total += folded(2.0 * value * value)
            damped = both + damping
            total += folded(jnp.where(diagonal, damped * damped, 2.0 * both * both))
            line = sorted_ref[half * 4, 2 * BIG + d:2 * BIG + d + 1, :] + damping
            total += jnp.where(
                lax.broadcasted_iota(jnp.int32, (8, SUB), 0) == 0, line * line, 0.0
            )
        for which in range(1, 4):
            value = sorted_ref[half * 4 + which, :2 * BIG, :]
            total += folded(2.0 * value * value)
    sums = jnp.sum(jnp.sum(total, axis=0, keepdims=True), axis=1, keepdims=True)
    frobenius = jnp.sqrt(sums)
    factor = 0.25 * newton_scale / frobenius
    scale = 1.0 / jnp.sqrt(jnp.sqrt(frobenius / newton_scale))
    shift = 1.25 - factor * damping

    def put(rows, cols, value, on_diagonal=False, keep=True):
        cross[rows, cols] = value
        first = -factor * value
        if on_diagonal:
            first += jnp.where(diagonal, shift, 0.0)
        if keep:
            mat[rows, cols] = first
        f_hi[rows, cols], f_lo[rows, cols] = split(first)

    for half in range(2):
        for d in range(2):
            at = 2 * half + d
            start = d * BIG
            value = sorted_ref[half * 4, start:start + SUB, :]
            put(sub(2 * at), sub(2 * at + 1), value)
            put(sub(2 * at + 1), sub(2 * at), value.T)
            both = sorted_ref[half * 4, start + SUB:start + BIG, :]
            flipped = both.T
            line = sorted_ref[half * 4, 2 * BIG + d:2 * BIG + d + 1, :]
            put(sub(2 * at), sub(2 * at), jnp.where(upper, both, flipped), True)
            second = jnp.where(
                diagonal,
                jnp.broadcast_to(line, (SUB, SUB)),
                jnp.where(upper, flipped, both),
            )
            put(sub(2 * at + 1), sub(2 * at + 1), second, True)
        for which in range(1, 4):
            row, col = OFF_BLOCKS[half][which - 1]
            for part in range(2):
                value = sorted_ref[half * 4 + which, part * BIG:(part + 1) * BIG, :]
                put(big(row), sub(2 * col + part), value)
                put(sub(2 * col + part), big(row), value.T, keep=False)
    stat_ref[...] = cross[pl.ds(pl.multiple_of(panel * 32, 32), 32), :]

    def dots(terms, rows, cols, done):
        middle = (rows.start + rows.stop) // 2
        for part in (slice(rows.start, middle), slice(middle, rows.stop)):
            done(
                part,
                sum(
                    jnp.dot(a[part, :], b[:, cols], preferred_element_type=jnp.float32)
                    for a, b in terms
                ),
            )

    def store(hi, lo, i, j, value):
        hi[big(i), big(j)], lo[big(i), big(j)] = split(value)
        if i != j:
            hi[big(j), big(i)], lo[big(j), big(i)] = split(value.T)

    def keep(ref, cols):
        def done(rows, value):
            ref[rows, cols] = value
        return done

    def squared(hi, lo, done):
        for j in range(4):
            dots([(hi, lo)], slice(0, ORDER), big(j), keep(cross, big(j)))
        for j in range(4):
            dots([(hi, hi)], slice(0, (j + 1) * BIG), big(j), keep(work, big(j)))
            for i in range(j + 1):
                value = work[big(i), big(j)]
                done(i, j, value + (cross[big(i), big(j)] + cross[big(j), big(i)].T))

    def square_done(i, j, part):
        store(q_hi, q_lo, i, j, part)
        store(t_hi, t_lo, i, j, 1.25 * mat[big(i), big(j)] - part)

    squared(f_hi, f_lo, square_done)
    squared(q_hi, q_lo, lambda i, j, part: store(f_hi, f_lo, i, j, part))
    for j in range(4):
        terms = [(f_hi, t_hi), (f_hi, t_lo), (f_lo, t_hi)]
        dots(terms, slice(0, (j + 1) * BIG), big(j), keep(work, big(j)))
        for i in range(j + 1):
            part = scale * (1.25 * mat[big(i), big(j)] - work[big(i), big(j)])
            store(q_hi, q_lo, i, j, part)
    copies = []
    for n in range(4):
        cols = slice(n * BIG, min((n + 1) * BIG, grad_ref.shape[1]))
        dots([(q_hi, grad_ref), (q_lo, grad_ref)], slice(0, ORDER), cols, keep(out_ref, cols))
        copies.append(
            pltpu.make_async_copy(out_ref.at[:, cols], out_hbm.at[:, cols], sem_out.at[n])
        )
        copies[-1].start()
    for copy in copies:
        copy.wait()


def local(gradient, stat_old):
    vmem = pl.BlockSpec(memory_space=pltpu.VMEM)
    anywhere = pl.BlockSpec(memory_space=pl.ANY)

    def kept(value):
        return pltpu.with_memory_space_constraint(value, pltpu.VMEM)

    packed = (pltpu.VMEM((2, CHUNK, SUB), jnp.float32),) * 2
    blocks = pltpu.VMEM((5, BIG, BIG), jnp.float32)
    limit = pltpu.CompilerParams(vmem_limit_bytes=8 << 20)
    *for_other, grad_kept, old_kept = pl.pallas_call(
        load_kernel,
        out_shape=packed
        + tuple(pltpu.VMEM(value.shape, value.dtype) for value in (gradient, stat_old)),
        in_specs=[anywhere] * 2,
        out_specs=(vmem,) * 4,
        scratch_shapes=[blocks, pltpu.SemaphoreType.DMA((2,))],
        compiler_params=limit,
        name="gram_other",
    )(*(pltpu.with_memory_space_constraint(value, pltpu.HBM) for value in (gradient, stat_old)))
    grad_kept = kept(grad_kept)

    def move(value, first=0, second=0, other=0):
        return lax.ppermute(value, PLANE, pairs(first, second, other))

    arrived = [move(value, other=1) for value in for_other]
    own = pl.pallas_call(
        lambda *refs: gram_kernel(0, *refs),
        out_shape=packed,
        in_specs=[vmem] * 2,
        out_specs=(vmem,) * 2,
        scratch_shapes=[blocks],
        compiler_params=limit,
        name="gram_own",
    )(grad_kept, kept(old_kept))

    sums = {}
    for mine, others, order in zip(own, arrived, ORDER_SENT):
        for slot, k in enumerate(order):
            sums[k] = mine[slot] + others[slot]
    for k in (2, 1, 3):
        sums[k] = move(sums[k], first=k)
    chunk = (sums[0] + sums[1]) + (sums[2] + sums[3])
    others = [move(chunk, second=k) for k in (2, 1, 3)]
    chunk = (chunk + others[0]) + (others[1] + others[2])
    mine = [chunk] + [move(chunk, first=k) for k in (2, 1, 3)]
    chunks = mine + [move(value, other=1) for value in mine]

    square = (ORDER, ORDER)
    return pl.pallas_call(
        root_kernel,
        out_shape=(
            jax.ShapeDtypeStruct(gradient.shape, jnp.float32),
            jax.ShapeDtypeStruct(stat_old.shape, jnp.float32),
        ),
        in_specs=[vmem] * 9,
        out_specs=(anywhere, vmem),
        scratch_shapes=[pltpu.VMEM((8, CHUNK, SUB), jnp.float32)]
        + [pltpu.VMEM(square, jnp.float32)] * 3
        + [pltpu.VMEM(square, jnp.bfloat16)] * 6
        + [
            pltpu.VMEM(gradient.shape, jnp.float32),
            pltpu.SemaphoreType.DMA((4,)),
        ],
        compiler_params=pltpu.CompilerParams(vmem_limit_bytes=44 << 20),
        name="root",
    )(*map(kept, chunks), grad_kept)


def solution(mesh):
    fine = Mesh(mesh.devices.reshape(8, 2, 4, 2, 2), ("row",) + PLANE)
    placed = (P("row", PLANE), P(("row",) + PLANE, None))
    return jax.shard_map(
        local, mesh=fine, in_specs=placed, out_specs=placed, check_vma=False
    )
```

```python
import jax
import jax.numpy as jnp
from jax import lax
from jax.experimental import pallas as pl
from jax.experimental.pallas import tpu as pltpu
from jax.sharding import Mesh, PartitionSpec as P

COLS = 28672
ORDER = 1024
BIG = 256
SUB = 128
PARTS = (BIG, BIG + 8)

damping = 0.001
stat_decay = 0.9
newton_scale = 2.5
weight_new = (1.0 - stat_decay) / COLS

ORIGINS = (0, 1, 3, 2)
PLANE = ("xh", "y", "core", "xl")


def pairs(first, second, other):
    found = []
    for x in range(4):
        for y in range(4):
            for core in range(2):
                dx, dy = (second, first) if core else (first, second)
                ends = []
                for u, v, w in ((x, y, core), ((x + dx) % 4, (y + dy) % 4, core ^ other)):
                    ends.append(((u // 2 * 4 + v) * 2 + w) * 2 + u % 2)
                found.append(tuple(ends))
    return found


def position():
    places = lax.axis_index("xh") * 2 + lax.axis_index("xl"), lax.axis_index("y")
    core = lax.axis_index("core")
    panel = (
        lax.axis_index("xh") * 16 + lax.axis_index("y") * 4 + core * 2 + lax.axis_index("xl")
    )
    return places, core, panel


OFF_BLOCKS = (((0, 1), (0, 2), (0, 3)), ((1, 2), (1, 3), (2, 3)))


def off_block(half, which):
    row = jnp.where(half == 0, 0, jnp.where(which == 3, 2, 1))
    col = jnp.where(half == 0, which, jnp.where(which == 1, 2, 3))
    return row, col


def sub_masks():
    rows = lax.broadcasted_iota(jnp.int32, (SUB, SUB), 0)
    cols = lax.broadcasted_iota(jnp.int32, (SUB, SUB), 1)
    return rows <= cols, rows == cols


def load_kernel(grad_hbm, old_hbm, left_ref, right_ref, grad_ref, old_ref, blocks, sems):
    copies = [
        pltpu.make_async_copy(grad_hbm, grad_ref, sems.at[0]),
        pltpu.make_async_copy(old_hbm, old_ref, sems.at[1]),
    ]
    for copy in copies:
        copy.start()
    for copy in copies:
        copy.wait()
    gram_kernel(1, grad_ref, old_ref, left_ref, right_ref, blocks)


def gram_kernel(flip, grad_ref, old_ref, left_ref, right_ref, blocks):
    places, core, panel = position()
    half = jnp.bitwise_xor(core, flip)
    place = jnp.where(half == 0, places[0], places[1])
    old_big = panel // 8
    old_row = pl.multiple_of((panel % 8) * 32, 32)
    upper, diagonal = sub_masks()

    def big(index):
        return pl.ds(pl.multiple_of(index * BIG, BIG), BIG)

    which = [(place + k) % 4 for k in range(4)]
    where = []
    for k in range(4):
        row, col = off_block(half, which[k])
        where.append(tuple(jnp.where(which[k] == 0, 2 * half, v) for v in (row, col)))
    where.append((2 * half + 1, 2 * half + 1))
    for n, (row, col) in enumerate(where):
        blocks[n] = weight_new * lax.dot_general(
            grad_ref[big(row), :],
            grad_ref[big(col), :],
            (((1,), (1,)), ((), ())),
            preferred_element_type=jnp.float32,
        )
    for n, (row, col) in enumerate(where):

        @pl.when(old_big == row)
        def _():
            blocks[n, pl.ds(old_row, 32), :] += stat_decay * old_ref[:, big(col)]

    for k in range(4):

        @pl.when(which[k] == 0)
        def _():
            extra = []
            for n, ref in ((k, left_ref), (4, right_ref)):
                second = blocks[n, SUB:, SUB:]
                ref[k, :SUB, :] = blocks[n, :SUB, SUB:]
                ref[k, SUB:BIG, :] = jnp.where(upper, blocks[n, :SUB, :SUB], second)
                extra.append(jnp.sum(jnp.where(diagonal, second, 0.0), axis=0, keepdims=True))
            right_ref[k, BIG:, :] = jnp.concatenate(
                extra + [jnp.zeros((6, SUB), jnp.float32)], axis=0
            )

        @pl.when(which[k] != 0)
        def _():
            left_ref[k] = blocks[k, :, :SUB]
            right_ref[k, :BIG, :] = blocks[k, :, SUB:]
            right_ref[k, BIG:, :] = jnp.zeros((8, SUB), jnp.float32)


def split(value):
    high = value.astype(jnp.bfloat16)
    return high, (value - high.astype(jnp.float32)).astype(jnp.bfloat16)


def big(i):
    return slice(i * BIG, (i + 1) * BIG)


def sub(i):
    return slice(i * SUB, (i + 1) * SUB)


def root_kernel(*refs):
    grad_ref, out_hbm, stat_ref = refs[16:19]
    sorted_ref, mat, cross, work, f_hi, f_lo, q_hi, q_lo, t_hi, t_lo, out_ref, sem_out = refs[19:]
    places, core, panel = position()
    upper, diagonal = sub_masks()

    for n in range(8):
        half = jnp.bitwise_xor(core, n // 4)
        which = (jnp.where(half == 0, places[0], places[1]) + 4 - ORIGINS[n % 4]) % 4
        chunk = half * 4 + which
        sorted_ref[chunk, :BIG, :] = refs[n][...]
        sorted_ref[chunk, BIG:, :] = refs[8 + n][...]

    total = jnp.zeros((8, SUB), jnp.float32)

    def folded(value):
        return jnp.sum(value.reshape(-1, 8, SUB), axis=0)

    for half in range(2):
        for d in range(2):
            start = d * BIG
            value = sorted_ref[half * 4, start:start + SUB, :]
            both = sorted_ref[half * 4, start + SUB:start + BIG, :]
            total += folded(2.0 * value * value)
            damped = both + damping
            total += folded(jnp.where(diagonal, damped * damped, 2.0 * both * both))
            line = sorted_ref[half * 4, 2 * BIG + d:2 * BIG + d + 1, :] + damping
            total += jnp.where(
                lax.broadcasted_iota(jnp.int32, (8, SUB), 0) == 0, line * line, 0.0
            )
        for which in range(1, 4):
            value = sorted_ref[half * 4 + which, :2 * BIG, :]
            total += folded(2.0 * value * value)
    sums = jnp.sum(jnp.sum(total, axis=0, keepdims=True), axis=1, keepdims=True)
    frobenius = jnp.sqrt(sums)
    factor = 0.25 * newton_scale / frobenius
    scale = 1.0 / jnp.sqrt(jnp.sqrt(frobenius / newton_scale))
    shift = 1.25 - factor * damping

    def put(rows, cols, value, on_diagonal=False, keep=True):
        cross[rows, cols] = value
        first = -factor * value
        if on_diagonal:
            first += jnp.where(diagonal, shift, 0.0)
        if keep:
            mat[rows, cols] = first
        f_hi[rows, cols], f_lo[rows, cols] = split(first)

    for half in range(2):
        for d in range(2):
            at = 2 * half + d
            start = d * BIG
            value = sorted_ref[half * 4, start:start + SUB, :]
            put(sub(2 * at), sub(2 * at + 1), value)
            put(sub(2 * at + 1), sub(2 * at), value.T)
            both = sorted_ref[half * 4, start + SUB:start + BIG, :]
            flipped = both.T
            line = sorted_ref[half * 4, 2 * BIG + d:2 * BIG + d + 1, :]
            put(sub(2 * at), sub(2 * at), jnp.where(upper, both, flipped), True)
            second = jnp.where(
                diagonal,
                jnp.broadcast_to(line, (SUB, SUB)),
                jnp.where(upper, flipped, both),
            )
            put(sub(2 * at + 1), sub(2 * at + 1), second, True)
        for which in range(1, 4):
            row, col = OFF_BLOCKS[half][which - 1]
            for part in range(2):
                value = sorted_ref[half * 4 + which, part * BIG:(part + 1) * BIG, :]
                put(big(row), sub(2 * col + part), value)
                put(sub(2 * col + part), big(row), value.T, keep=False)
    stat_ref[...] = cross[pl.ds(pl.multiple_of(panel * 32, 32), 32), :]

    def dots(terms, rows, cols, done):
        middle = (rows.start + rows.stop) // 2
        for part in (slice(rows.start, middle), slice(middle, rows.stop)):
            done(
                part,
                sum(
                    jnp.dot(a[part, :], b[:, cols], preferred_element_type=jnp.float32)
                    for a, b in terms
                ),
            )

    def store(hi, lo, i, j, value):
        hi[big(i), big(j)], lo[big(i), big(j)] = split(value)
        if i != j:
            hi[big(j), big(i)], lo[big(j), big(i)] = split(value.T)

    def keep(ref, cols):
        def done(rows, value):
            ref[rows, cols] = value
        return done

    def squared(hi, lo, done):
        for j in range(4):
            dots([(hi, lo)], slice(0, ORDER), big(j), keep(cross, big(j)))
        for j in range(4):
            dots([(hi, hi)], slice(0, (j + 1) * BIG), big(j), keep(work, big(j)))
            for i in range(j + 1):
                value = work[big(i), big(j)]
                done(i, j, value + (cross[big(i), big(j)] + cross[big(j), big(i)].T))

    def square_done(i, j, part):
        store(q_hi, q_lo, i, j, part)
        store(t_hi, t_lo, i, j, 1.25 * mat[big(i), big(j)] - part)

    squared(f_hi, f_lo, square_done)
    squared(q_hi, q_lo, lambda i, j, part: store(f_hi, f_lo, i, j, part))
    for j in range(4):
        terms = [(f_hi, t_hi), (f_hi, t_lo), (f_lo, t_hi)]
        dots(terms, slice(0, (j + 1) * BIG), big(j), keep(work, big(j)))
        for i in range(j + 1):
            part = scale * (1.25 * mat[big(i), big(j)] - work[big(i), big(j)])
            store(q_hi, q_lo, i, j, part)
    copies = []
    for n in range(4):
        cols = slice(n * BIG, min((n + 1) * BIG, grad_ref.shape[1]))
        dots([(q_hi, grad_ref), (q_lo, grad_ref)], slice(0, ORDER), cols, keep(out_ref, cols))
        copies.append(
            pltpu.make_async_copy(out_ref.at[:, cols], out_hbm.at[:, cols], sem_out.at[n])
        )
        copies[-1].start()
    for copy in copies:
        copy.wait()


def local(gradient, stat_old):
    vmem = pl.BlockSpec(memory_space=pltpu.VMEM)
    anywhere = pl.BlockSpec(memory_space=pl.ANY)

    def kept(value):
        return pltpu.with_memory_space_constraint(value, pltpu.VMEM)

    packed = tuple(pltpu.VMEM((4, rows, SUB), jnp.float32) for rows in PARTS)
    blocks = pltpu.VMEM((5, BIG, BIG), jnp.float32)
    limit = pltpu.CompilerParams(vmem_limit_bytes=8 << 20)
    *for_other, grad_kept, old_kept = pl.pallas_call(
        load_kernel,
        out_shape=packed
        + tuple(pltpu.VMEM(value.shape, value.dtype) for value in (gradient, stat_old)),
        in_specs=[anywhere] * 2,
        out_specs=(vmem,) * 4,
        scratch_shapes=[blocks, pltpu.SemaphoreType.DMA((2,))],
        compiler_params=limit,
        name="gram_other",
    )(*(pltpu.with_memory_space_constraint(value, pltpu.HBM) for value in (gradient, stat_old)))
    grad_kept = kept(grad_kept)

    def move(value, first=0, second=0, other=0):
        return lax.ppermute(value, PLANE, pairs(first, second, other))

    arrived = [move(value, other=1) for value in for_other]
    own = pl.pallas_call(
        lambda *refs: gram_kernel(0, *refs),
        out_shape=packed,
        in_specs=[vmem] * 2,
        out_specs=(vmem,) * 2,
        scratch_shapes=[blocks],
        compiler_params=limit,
        name="gram_own",
    )(grad_kept, kept(old_kept))

    mine, theirs = [], []
    for part in range(2):
        sums = [own[part][k] + arrived[part][k] for k in range(4)]
        for k in (1, 3, 2):
            sums[k] = move(sums[k], first=k)
        chunk = (sums[0] + sums[1]) + (sums[2] + sums[3])
        others = [move(chunk, second=k) for k in (1, 3, 2)]
        chunk = (chunk + others[0]) + (others[1] + others[2])
        gathered = [chunk] + [move(chunk, first=k) for k in (1, 3, 2)]
        mine.append(gathered)
        theirs.append([move(value, other=1) for value in gathered])
    chunks = mine[0] + theirs[0] + mine[1] + theirs[1]

    square = (ORDER, ORDER)
    return pl.pallas_call(
        root_kernel,
        out_shape=(
            jax.ShapeDtypeStruct(gradient.shape, jnp.float32),
            jax.ShapeDtypeStruct(stat_old.shape, jnp.float32),
        ),
        in_specs=[vmem] * 17,
        out_specs=(anywhere, vmem),
        scratch_shapes=[pltpu.VMEM((8, sum(PARTS), SUB), jnp.float32)]
        + [pltpu.VMEM(square, jnp.float32)] * 3
        + [pltpu.VMEM(square, jnp.bfloat16)] * 6
        + [
            pltpu.VMEM(gradient.shape, jnp.float32),
            pltpu.SemaphoreType.DMA((4,)),
        ],
        compiler_params=pltpu.CompilerParams(vmem_limit_bytes=44 << 20),
        name="root",
    )(*map(kept, chunks), grad_kept)


def solution(mesh):
    fine = Mesh(mesh.devices.reshape(8, 2, 4, 2, 2), ("row",) + PLANE)
    placed = (P("row", PLANE), P(("row",) + PLANE, None))
    return jax.shard_map(
        local, mesh=fine, in_specs=placed, out_specs=placed, check_vma=False
    )
```

```python
import jax
import jax.numpy as jnp
from jax import lax
from jax.experimental import pallas as pl
from jax.experimental.pallas import tpu as pltpu
from jax.sharding import Mesh, PartitionSpec as P

COLS = 28672
ORDER = 1024
BIG = 256
SUB = 128
PARTS = (BIG, BIG + 8)

damping = 0.001
stat_decay = 0.9
newton_scale = 2.5
weight_new = (1.0 - stat_decay) / COLS

ORIGINS = (0, 2, 1, 3)
PLANE = ("xh", "y", "core", "xl")


def pairs(first, second, other):
    found = []
    for x in range(4):
        for y in range(4):
            for core in range(2):
                dx, dy = (first, second) if core else (second, first)
                ends = []
                for u, v, w in ((x, y, core), ((x + dx) % 4, (y + dy) % 4, core ^ other)):
                    ends.append(((u // 2 * 4 + v) * 2 + w) * 2 + u % 2)
                found.append(tuple(ends))
    return found


def position():
    places = lax.axis_index("y"), lax.axis_index("xh") * 2 + lax.axis_index("xl")
    core = lax.axis_index("core")
    panel = (
        lax.axis_index("xh") * 16 + lax.axis_index("y") * 4 + core * 2 + lax.axis_index("xl")
    )
    return places, core, panel


OFF_BLOCKS = (((0, 1), (0, 2), (0, 3)), ((1, 2), (1, 3), (2, 3)))


def off_block(half, which):
    row = jnp.where(half == 0, 0, jnp.where(which == 3, 2, 1))
    col = jnp.where(half == 0, which, jnp.where(which == 1, 2, 3))
    return row, col


def sub_masks():
    rows = lax.broadcasted_iota(jnp.int32, (SUB, SUB), 0)
    cols = lax.broadcasted_iota(jnp.int32, (SUB, SUB), 1)
    return rows <= cols, rows == cols


def load_kernel(grad_hbm, old_hbm, left_ref, right_ref, grad_ref, old_ref, blocks, sems):
    copies = [
        pltpu.make_async_copy(
            grad_hbm.at[i * BIG:(i + 1) * BIG, :], grad_ref.at[i * BIG:(i + 1) * BIG, :], sems.at[i]
        )
        for i in range(4)
    ] + [pltpu.make_async_copy(old_hbm, old_ref, sems.at[4])]
    for copy in copies:
        copy.start()
    for copy in copies:
        copy.wait()
    gram_kernel(1, grad_ref, old_ref, left_ref, right_ref, blocks)


def gram_kernel(flip, grad_ref, old_ref, left_ref, right_ref, blocks):
    places, core, panel = position()
    half = jnp.bitwise_xor(core, flip)
    place = jnp.where(half == 0, places[0], places[1])
    old_big = panel // 8
    old_row = pl.multiple_of((panel % 8) * 32, 32)
    upper, diagonal = sub_masks()

    def big(index):
        return pl.ds(pl.multiple_of(index * BIG, BIG), BIG)

    which = [(place + k) % 4 for k in range(4)]
    where = []
    for k in range(4):
        row, col = off_block(half, which[k])
        where.append(tuple(jnp.where(which[k] == 0, 2 * half, v) for v in (row, col)))
    where.append((2 * half + 1, 2 * half + 1))
    for n, (row, col) in enumerate(where):
        blocks[n] = weight_new * lax.dot_general(
            grad_ref[big(row), :],
            grad_ref[big(col), :],
            (((1,), (1,)), ((), ())),
            preferred_element_type=jnp.float32,
        )
    for n, (row, col) in enumerate(where):

        @pl.when(old_big == row)
        def _():
            blocks[n, pl.ds(old_row, 32), :] += stat_decay * old_ref[:, big(col)]

    for k in range(4):

        @pl.when(which[k] == 0)
        def _():
            extra = []
            for n, ref in ((k, left_ref), (4, right_ref)):
                second = blocks[n, SUB:, SUB:]
                ref[k, :SUB, :] = blocks[n, :SUB, SUB:]
                ref[k, SUB:BIG, :] = jnp.where(upper, blocks[n, :SUB, :SUB], second)
                extra.append(jnp.sum(jnp.where(diagonal, second, 0.0), axis=0, keepdims=True))
            right_ref[k, BIG:, :] = jnp.concatenate(
                extra + [jnp.zeros((6, SUB), jnp.float32)], axis=0
            )

        @pl.when(which[k] != 0)
        def _():
            left_ref[k] = blocks[k, :, :SUB]
            right_ref[k, :BIG, :] = blocks[k, :, SUB:]
            right_ref[k, BIG:, :] = jnp.zeros((8, SUB), jnp.float32)


def split(value):
    high = value.astype(jnp.bfloat16)
    return high, (value - high.astype(jnp.float32)).astype(jnp.bfloat16)


def big(i):
    return slice(i * BIG, (i + 1) * BIG)


def sub(i):
    return slice(i * SUB, (i + 1) * SUB)


def root_kernel(*refs):
    grad_ref, out_hbm, stat_hbm = refs[16:19]
    sorted_ref, mat, cross, work, f_hi, f_lo, q_hi, q_lo, t_hi, t_lo, out_ref, stat_ref, sem_out = refs[19:]
    places, core, panel = position()
    upper, diagonal = sub_masks()

    for n in range(8):
        half = jnp.bitwise_xor(core, n // 4)
        which = (jnp.where(half == 0, places[0], places[1]) + 4 - ORIGINS[n % 4]) % 4
        chunk = half * 4 + which
        sorted_ref[chunk, :BIG, :] = refs[n][...]
        sorted_ref[chunk, BIG:, :] = refs[8 + n][...]

    total = jnp.zeros((8, SUB), jnp.float32)

    def folded(value):
        return jnp.sum(value.reshape(-1, 8, SUB), axis=0)

    for half in range(2):
        for d in range(2):
            start = d * BIG
            value = sorted_ref[half * 4, start:start + SUB, :]
            both = sorted_ref[half * 4, start + SUB:start + BIG, :]
            total += folded(2.0 * value * value)
            damped = both + damping
            total += folded(jnp.where(diagonal, damped * damped, 2.0 * both * both))
            line = sorted_ref[half * 4, 2 * BIG + d:2 * BIG + d + 1, :] + damping
            total += jnp.where(
                lax.broadcasted_iota(jnp.int32, (8, SUB), 0) == 0, line * line, 0.0
            )
        for which in range(1, 4):
            value = sorted_ref[half * 4 + which, :2 * BIG, :]
            total += folded(2.0 * value * value)
    sums = jnp.sum(jnp.sum(total, axis=0, keepdims=True), axis=1, keepdims=True)
    frobenius = jnp.sqrt(sums)
    factor = 0.25 * newton_scale / frobenius
    scale = 1.0 / jnp.sqrt(jnp.sqrt(frobenius / newton_scale))
    shift = 1.25 - factor * damping

    def put(rows, cols, value, on_diagonal=False, keep=True):
        cross[rows, cols] = value
        first = -factor * value
        if on_diagonal:
            first += jnp.where(diagonal, shift, 0.0)
        if keep:
            mat[rows, cols] = first
        f_hi[rows, cols], f_lo[rows, cols] = split(first)

    for half in range(2):
        for d in range(2):
            at = 2 * half + d
            start = d * BIG
            value = sorted_ref[half * 4, start:start + SUB, :]
            put(sub(2 * at), sub(2 * at + 1), value)
            put(sub(2 * at + 1), sub(2 * at), value.T)
            both = sorted_ref[half * 4, start + SUB:start + BIG, :]
            flipped = both.T
            line = sorted_ref[half * 4, 2 * BIG + d:2 * BIG + d + 1, :]
            put(sub(2 * at), sub(2 * at), jnp.where(upper, both, flipped), True)
            second = jnp.where(
                diagonal,
                jnp.broadcast_to(line, (SUB, SUB)),
                jnp.where(upper, flipped, both),
            )
            put(sub(2 * at + 1), sub(2 * at + 1), second, True)
        for which in range(1, 4):
            row, col = OFF_BLOCKS[half][which - 1]
            for part in range(2):
                value = sorted_ref[half * 4 + which, part * BIG:(part + 1) * BIG, :]
                put(big(row), sub(2 * col + part), value)
                put(sub(2 * col + part), big(row), value.T, keep=False)
    stat_ref[...] = cross[pl.ds(pl.multiple_of(panel * 32, 32), 32), :]
    copies = [pltpu.make_async_copy(stat_ref, stat_hbm, sem_out.at[4])]
    copies[0].start()

    def dots(terms, rows, cols, done):
        middle = (rows.start + rows.stop) // 2
        for part in (slice(rows.start, middle), slice(middle, rows.stop)):
            done(
                part,
                sum(
                    jnp.dot(a[part, :], b[:, cols], preferred_element_type=jnp.float32)
                    for a, b in terms
                ),
            )

    def store(hi, lo, i, j, value):
        hi[big(i), big(j)], lo[big(i), big(j)] = split(value)
        if i != j:
            hi[big(j), big(i)], lo[big(j), big(i)] = split(value.T)

    def keep(ref, cols):
        def done(rows, value):
            ref[rows, cols] = value
        return done

    def squared(hi, lo, done):
        for j in range(4):
            dots([(hi, lo)], slice(0, ORDER), big(j), keep(cross, big(j)))
        for j in range(4):
            dots([(hi, hi)], slice(0, (j + 1) * BIG), big(j), keep(work, big(j)))
            for i in range(j + 1):
                value = work[big(i), big(j)]
                done(i, j, value + (cross[big(i), big(j)] + cross[big(j), big(i)].T))

    def square_done(i, j, part):
        store(q_hi, q_lo, i, j, part)
        store(t_hi, t_lo, i, j, 1.25 * mat[big(i), big(j)] - part)

    squared(f_hi, f_lo, square_done)
    squared(q_hi, q_lo, lambda i, j, part: store(f_hi, f_lo, i, j, part))
    for j in range(4):
        terms = [(f_hi, t_hi), (f_hi, t_lo), (f_lo, t_hi)]
        dots(terms, slice(0, (j + 1) * BIG), big(j), keep(work, big(j)))
        for i in range(j + 1):
            part = scale * (1.25 * mat[big(i), big(j)] - work[big(i), big(j)])
            store(q_hi, q_lo, i, j, part)
    for n in range(4):
        cols = slice(n * BIG, min((n + 1) * BIG, grad_ref.shape[1]))
        dots([(q_hi, grad_ref), (q_lo, grad_ref)], slice(0, ORDER), cols, keep(out_ref, cols))
        copies.append(
            pltpu.make_async_copy(out_ref.at[:, cols], out_hbm.at[:, cols], sem_out.at[n])
        )
        copies[-1].start()
    for copy in copies:
        copy.wait()


def local(gradient, stat_old):
    vmem = pl.BlockSpec(memory_space=pltpu.VMEM)
    anywhere = pl.BlockSpec(memory_space=pl.ANY)

    def kept(value):
        return pltpu.with_memory_space_constraint(value, pltpu.VMEM)

    packed = tuple(pltpu.VMEM((4, rows, SUB), jnp.float32) for rows in PARTS)
    blocks = pltpu.VMEM((5, BIG, BIG), jnp.float32)
    limit = pltpu.CompilerParams(vmem_limit_bytes=8 << 20)
    *for_other, grad_kept, old_kept = pl.pallas_call(
        load_kernel,
        out_shape=packed
        + tuple(pltpu.VMEM(value.shape, value.dtype) for value in (gradient, stat_old)),
        in_specs=[anywhere] * 2,
        out_specs=(vmem,) * 4,
        scratch_shapes=[blocks, pltpu.SemaphoreType.DMA((5,))],
        compiler_params=limit,
        name="gram_other",
    )(*(pltpu.with_memory_space_constraint(value, pltpu.HBM) for value in (gradient, stat_old)))
    grad_kept = kept(grad_kept)

    def move(value, first=0, second=0, other=0):
        return lax.ppermute(value, PLANE, pairs(first, second, other))

    arrived = [move(value, other=1) for value in for_other]
    own = pl.pallas_call(
        lambda *refs: gram_kernel(0, *refs),
        out_shape=packed,
        in_specs=[vmem] * 2,
        out_specs=(vmem,) * 2,
        scratch_shapes=[blocks],
        compiler_params=limit,
        name="gram_own",
    )(grad_kept, kept(old_kept))

    mine, theirs = [], []
    for part in range(2):
        sums = [own[part][k] + arrived[part][k] for k in range(4)]
        for k in (2, 1, 3):
            sums[k] = move(sums[k], first=k)
        chunk = (sums[0] + sums[1]) + (sums[2] + sums[3])
        others = [move(chunk, second=k) for k in (2, 1, 3)]
        chunk = (chunk + others[0]) + (others[1] + others[2])
        gathered = [chunk] + [move(chunk, first=k) for k in (2, 1, 3)]
        mine.append(gathered)
        theirs.append([move(value, other=1) for value in gathered])
    chunks = mine[0] + theirs[0] + mine[1] + theirs[1]

    square = (ORDER, ORDER)
    return pl.pallas_call(
        root_kernel,
        out_shape=(
            jax.ShapeDtypeStruct(gradient.shape, jnp.float32),
            jax.ShapeDtypeStruct(stat_old.shape, jnp.float32),
        ),
        in_specs=[vmem] * 17,
        out_specs=(anywhere, anywhere),
        scratch_shapes=[pltpu.VMEM((8, sum(PARTS), SUB), jnp.float32)]
        + [pltpu.VMEM(square, jnp.float32)] * 3
        + [pltpu.VMEM(square, jnp.bfloat16)] * 6
        + [
            pltpu.VMEM(gradient.shape, jnp.float32),
            pltpu.VMEM(stat_old.shape, jnp.float32),
            pltpu.SemaphoreType.DMA((5,)),
        ],
        compiler_params=pltpu.CompilerParams(vmem_limit_bytes=44 << 20),
        name="root",
    )(*map(kept, chunks), grad_kept)


def solution(mesh):
    fine = Mesh(mesh.devices.reshape(8, 2, 4, 2, 2), ("row",) + PLANE)
    placed = (P("row", PLANE), P(("row",) + PLANE, None))
    return jax.shard_map(
        local, mesh=fine, in_specs=placed, out_specs=placed, check_vma=False
    )
```

```python
import jax
import jax.numpy as jnp
from jax import lax
from jax.experimental import pallas as pl
from jax.experimental.pallas import tpu as pltpu
from jax.sharding import Mesh, PartitionSpec as P

COLS = 28672
ORDER = 1024
BIG = 256
SUB = 128
PARTS = (BIG, BIG + 8)

damping = 0.001
stat_decay = 0.9
newton_scale = 2.5
weight_new = (1.0 - stat_decay) / COLS

ORIGINS = (0, 2, 1, 3)
PLANE = ("xh", "y", "core", "xl")


def pairs(first, second, other):
    found = []
    for x in range(4):
        for y in range(4):
            for core in range(2):
                dx, dy = (first, second) if core else (second, first)
                ends = []
                for u, v, w in ((x, y, core), ((x + dx) % 4, (y + dy) % 4, core ^ other)):
                    ends.append(((u // 2 * 4 + v) * 2 + w) * 2 + u % 2)
                found.append(tuple(ends))
    return found


def position():
    places = lax.axis_index("y"), lax.axis_index("xh") * 2 + lax.axis_index("xl")
    core = lax.axis_index("core")
    panel = (
        lax.axis_index("xh") * 16 + lax.axis_index("y") * 4 + core * 2 + lax.axis_index("xl")
    )
    return places, core, panel


OFF_BLOCKS = (((0, 1), (0, 2), (0, 3)), ((1, 2), (1, 3), (2, 3)))


def off_block(half, which):
    row = jnp.where(half == 0, 0, jnp.where(which == 3, 2, 1))
    col = jnp.where(half == 0, which, jnp.where(which == 1, 2, 3))
    return row, col


def sub_masks():
    rows = lax.broadcasted_iota(jnp.int32, (SUB, SUB), 0)
    cols = lax.broadcasted_iota(jnp.int32, (SUB, SUB), 1)
    return rows <= cols, rows == cols


def load_kernel(grad_hbm, old_hbm, left_ref, right_ref, grad_ref, old_ref, blocks, sems):
    copies = [
        pltpu.make_async_copy(
            grad_hbm.at[i * BIG:(i + 1) * BIG, :], grad_ref.at[i * BIG:(i + 1) * BIG, :], sems.at[i]
        )
        for i in range(4)
    ] + [pltpu.make_async_copy(old_hbm, old_ref, sems.at[4])]
    for copy in copies:
        copy.start()
    for copy in copies:
        copy.wait()
    gram_kernel(1, grad_ref, old_ref, left_ref, right_ref, blocks)


def gram_kernel(flip, grad_ref, old_ref, left_ref, right_ref, blocks):
    places, core, panel = position()
    half = jnp.bitwise_xor(core, flip)
    place = jnp.where(half == 0, places[0], places[1])
    old_big = panel // 8
    old_row = pl.multiple_of((panel % 8) * 32, 32)
    upper, diagonal = sub_masks()

    def big(index):
        return pl.ds(pl.multiple_of(index * BIG, BIG), BIG)

    which = [(place + k) % 4 for k in range(4)]
    where = []
    for k in range(4):
        row, col = off_block(half, which[k])
        where.append(tuple(jnp.where(which[k] == 0, 2 * half, v) for v in (row, col)))
    where.append((2 * half + 1, 2 * half + 1))
    for n, (row, col) in enumerate(where):
        blocks[n] = weight_new * lax.dot_general(
            grad_ref[big(row), :],
            grad_ref[big(col), :],
            (((1,), (1,)), ((), ())),
            preferred_element_type=jnp.float32,
        )
    for n, (row, col) in enumerate(where):

        @pl.when(old_big == row)
        def _():
            blocks[n, pl.ds(old_row, 32), :] += stat_decay * old_ref[:, big(col)]

    for k in range(4):

        @pl.when(which[k] == 0)
        def _():
            extra = []
            for n, ref in ((k, left_ref), (4, right_ref)):
                second = blocks[n, SUB:, SUB:]
                ref[k, :SUB, :] = blocks[n, :SUB, SUB:]
                ref[k, SUB:BIG, :] = jnp.where(upper, blocks[n, :SUB, :SUB], second)
                extra.append(jnp.sum(jnp.where(diagonal, second, 0.0), axis=0, keepdims=True))
            right_ref[k, BIG:, :] = jnp.concatenate(
                extra + [jnp.zeros((6, SUB), jnp.float32)], axis=0
            )

        @pl.when(which[k] != 0)
        def _():
            left_ref[k] = blocks[k, :, :SUB]
            right_ref[k, :BIG, :] = blocks[k, :, SUB:]
            right_ref[k, BIG:, :] = jnp.zeros((8, SUB), jnp.float32)


def split(value):
    high = value.astype(jnp.bfloat16)
    return high, (value - high.astype(jnp.float32)).astype(jnp.bfloat16)


def big(i):
    return slice(i * BIG, (i + 1) * BIG)


def sub(i):
    return slice(i * SUB, (i + 1) * SUB)


def root_kernel(*refs):
    grad_ref, out_hbm, stat_hbm = refs[16:19]
    sorted_ref, mat, cross, work, f_hi, f_lo, q_hi, q_lo, t_hi, t_lo, out_ref, stat_ref, sem_out = refs[19:]
    places, core, panel = position()
    upper, diagonal = sub_masks()

    for n in range(8):
        half = jnp.bitwise_xor(core, n // 4)
        which = (jnp.where(half == 0, places[0], places[1]) + 4 - ORIGINS[n % 4]) % 4
        chunk = half * 4 + which
        sorted_ref[chunk, :BIG, :] = refs[n][...]
        sorted_ref[chunk, BIG:, :] = refs[8 + n][...]

    total = jnp.zeros((8, SUB), jnp.float32)

    def folded(value):
        return jnp.sum(value.reshape(-1, 8, SUB), axis=0)

    for half in range(2):
        for d in range(2):
            start = d * BIG
            value = sorted_ref[half * 4, start:start + SUB, :]
            both = sorted_ref[half * 4, start + SUB:start + BIG, :]
            total += folded(2.0 * value * value)
            damped = both + damping
            total += folded(jnp.where(diagonal, damped * damped, 2.0 * both * both))
            line = sorted_ref[half * 4, 2 * BIG + d:2 * BIG + d + 1, :] + damping
            total += jnp.where(
                lax.broadcasted_iota(jnp.int32, (8, SUB), 0) == 0, line * line, 0.0
            )
        for which in range(1, 4):
            value = sorted_ref[half * 4 + which, :2 * BIG, :]
            total += folded(2.0 * value * value)
    sums = jnp.sum(jnp.sum(total, axis=0, keepdims=True), axis=1, keepdims=True)
    frobenius = jnp.sqrt(sums)
    factor = 0.25 * newton_scale / frobenius
    scale = 1.0 / jnp.sqrt(jnp.sqrt(frobenius / newton_scale))
    shift = 1.25 - factor * damping

    def put(rows, cols, value, on_diagonal=False, keep=True):
        cross[rows, cols] = value
        first = -factor * value
        if on_diagonal:
            first += jnp.where(diagonal, shift, 0.0)
        if keep:
            mat[rows, cols] = first
        f_hi[rows, cols], f_lo[rows, cols] = split(first)

    for half in range(2):
        for d in range(2):
            at = 2 * half + d
            start = d * BIG
            value = sorted_ref[half * 4, start:start + SUB, :]
            put(sub(2 * at), sub(2 * at + 1), value)
            put(sub(2 * at + 1), sub(2 * at), value.T)
            both = sorted_ref[half * 4, start + SUB:start + BIG, :]
            flipped = both.T
            line = sorted_ref[half * 4, 2 * BIG + d:2 * BIG + d + 1, :]
            put(sub(2 * at), sub(2 * at), jnp.where(upper, both, flipped), True)
            second = jnp.where(
                diagonal,
                jnp.broadcast_to(line, (SUB, SUB)),
                jnp.where(upper, flipped, both),
            )
            put(sub(2 * at + 1), sub(2 * at + 1), second, True)
        for which in range(1, 4):
            row, col = OFF_BLOCKS[half][which - 1]
            for part in range(2):
                value = sorted_ref[half * 4 + which, part * BIG:(part + 1) * BIG, :]
                put(big(row), sub(2 * col + part), value)
                put(sub(2 * col + part), big(row), value.T, keep=False)
    stat_ref[...] = cross[pl.ds(pl.multiple_of(panel * 32, 32), 32), :]
    copies = [pltpu.make_async_copy(stat_ref, stat_hbm, sem_out.at[4])]
    copies[0].start()

    def dots(terms, rows, cols, done):
        middle = (rows.start + rows.stop) // 2
        for part in (slice(rows.start, middle), slice(middle, rows.stop)):
            done(
                part,
                sum(
                    jnp.dot(a[part, :], b[:, cols], preferred_element_type=jnp.float32)
                    for a, b in terms
                ),
            )

    def store(hi, lo, i, j, value):
        hi[big(i), big(j)], lo[big(i), big(j)] = split(value)
        if i != j:
            hi[big(j), big(i)], lo[big(j), big(i)] = split(value.T)

    def keep(ref, cols):
        def done(rows, value):
            ref[rows, cols] = value
        return done

    def squared(hi, lo, done):
        for j in range(4):
            dots([(hi, lo)], slice(0, ORDER), big(j), keep(cross, big(j)))
        for j in range(4):
            dots([(hi, hi)], slice(0, (j + 1) * BIG), big(j), keep(work, big(j)))
            for i in range(j + 1):
                value = work[big(i), big(j)]
                done(i, j, value + (cross[big(i), big(j)] + cross[big(j), big(i)].T))

    def square_done(i, j, part):
        store(q_hi, q_lo, i, j, part)
        store(t_hi, t_lo, i, j, 1.25 * mat[big(i), big(j)] - part)

    squared(f_hi, f_lo, square_done)
    squared(q_hi, q_lo, lambda i, j, part: store(f_hi, f_lo, i, j, part))
    for j in range(4):
        terms = [(f_hi, t_hi), (f_hi, t_lo), (f_lo, t_hi)]
        dots(terms, slice(0, (j + 1) * BIG), big(j), keep(work, big(j)))
        for i in range(j + 1):
            part = scale * (1.25 * mat[big(i), big(j)] - work[big(i), big(j)])
            store(q_hi, q_lo, i, j, part)
    for n in range(4):
        cols = slice(n * BIG, min((n + 1) * BIG, grad_ref.shape[1]))
        dots([(q_hi, grad_ref), (q_lo, grad_ref)], slice(0, ORDER), cols, keep(out_ref, cols))
        for part in range(2):
            rows = slice(part * ORDER // 2, (part + 1) * ORDER // 2)
            copies.append(
                pltpu.make_async_copy(
                    out_ref.at[rows, cols], out_hbm.at[rows, cols], sem_out.at[5 + 2 * n + part]
                )
            )
            copies[-1].start()
    for copy in copies:
        copy.wait()


def local(gradient, stat_old):
    vmem = pl.BlockSpec(memory_space=pltpu.VMEM)
    anywhere = pl.BlockSpec(memory_space=pl.ANY)

    def kept(value):
        return pltpu.with_memory_space_constraint(value, pltpu.VMEM)

    packed = tuple(pltpu.VMEM((4, rows, SUB), jnp.float32) for rows in PARTS)
    blocks = pltpu.VMEM((5, BIG, BIG), jnp.float32)
    limit = pltpu.CompilerParams(vmem_limit_bytes=8 << 20)
    *for_other, grad_kept, old_kept = pl.pallas_call(
        load_kernel,
        out_shape=packed
        + tuple(pltpu.VMEM(value.shape, value.dtype) for value in (gradient, stat_old)),
        in_specs=[anywhere] * 2,
        out_specs=(vmem,) * 4,
        scratch_shapes=[blocks, pltpu.SemaphoreType.DMA((5,))],
        compiler_params=limit,
        name="gram_other",
    )(*(pltpu.with_memory_space_constraint(value, pltpu.HBM) for value in (gradient, stat_old)))
    grad_kept = kept(grad_kept)

    def move(value, first=0, second=0, other=0):
        return lax.ppermute(value, PLANE, pairs(first, second, other))

    arrived = [move(value, other=1) for value in for_other]
    own = pl.pallas_call(
        lambda *refs: gram_kernel(0, *refs),
        out_shape=packed,
        in_specs=[vmem] * 2,
        out_specs=(vmem,) * 2,
        scratch_shapes=[blocks],
        compiler_params=limit,
        name="gram_own",
    )(grad_kept, kept(old_kept))

    mine, theirs = [], []
    for part in range(2):
        sums = [own[part][k] + arrived[part][k] for k in range(4)]
        for k in (2, 1, 3):
            sums[k] = move(sums[k], first=k)
        chunk = (sums[0] + sums[1]) + (sums[2] + sums[3])
        others = [move(chunk, second=k) for k in (2, 1, 3)]
        chunk = (chunk + others[0]) + (others[1] + others[2])
        gathered = [chunk] + [move(chunk, first=k) for k in (2, 1, 3)]
        mine.append(gathered)
        theirs.append([move(value, other=1) for value in gathered])
    chunks = mine[0] + theirs[0] + mine[1] + theirs[1]

    square = (ORDER, ORDER)
    return pl.pallas_call(
        root_kernel,
        out_shape=(
            jax.ShapeDtypeStruct(gradient.shape, jnp.float32),
            jax.ShapeDtypeStruct(stat_old.shape, jnp.float32),
        ),
        in_specs=[vmem] * 17,
        out_specs=(anywhere, anywhere),
        scratch_shapes=[pltpu.VMEM((8, sum(PARTS), SUB), jnp.float32)]
        + [pltpu.VMEM(square, jnp.float32)] * 3
        + [pltpu.VMEM(square, jnp.bfloat16)] * 6
        + [
            pltpu.VMEM(gradient.shape, jnp.float32),
            pltpu.VMEM(stat_old.shape, jnp.float32),
            pltpu.SemaphoreType.DMA((13,)),
        ],
        compiler_params=pltpu.CompilerParams(vmem_limit_bytes=44 << 20),
        name="root",
    )(*map(kept, chunks), grad_kept)


def solution(mesh):
    fine = Mesh(mesh.devices.reshape(8, 2, 4, 2, 2), ("row",) + PLANE)
    placed = (P("row", PLANE), P(("row",) + PLANE, None))
    return jax.shard_map(
        local, mesh=fine, in_specs=placed, out_specs=placed, check_vma=False
    )
```
